32 devices in a mesh: row: 4 (over x, core), col: 8 (over z, y).
Axes of the slice: x: 2, y: 2, z: 4, core: 2. Of those that a mesh axis runs over, the one named last changes fastest.
Arguments:
- points: bfloat16 [65536, 256], P(('row', 'col')), may hold values from -6 to 6
- rotated_slot: int32 [65536], P(('row', 'col')), may hold values from 0 to 65535, as said below
- fine_attend_in: bfloat16 [2, 256, 768], replicated, may hold values from -8 to 8
- fine_attend_out: bfloat16 [2, 256, 256], replicated, may hold values from -0.375 to 0.375
- fine_gate_up: bfloat16 [2, 256, 2048], replicated, may hold values from -0.375 to 0.375
- fine_down: bfloat16 [2, 1024, 256], replicated, may hold values from -0.1875 to 0.1875
- pool_weight: bfloat16 [2048, 512], replicated, may hold values from -0.125 to 0.125
- coarse_attend_in: bfloat16 [512, 1536], replicated, may hold values from -8 to 8
- coarse_attend_out: bfloat16 [512, 512], replicated, may hold values from -0.25 to 0.25
- coarse_gate_up: bfloat16 [512, 4096], replicated, may hold values from -0.25 to 0.25
- coarse_down: bfloat16 [2048, 512], replicated, may hold values from -0.125 to 0.125
- unpool_weight: bfloat16 [512, 2048], replicated, may hold values from -0.25 to 0.25
Outputs:
- refined: bfloat16 [65536, 256], P(('row', 'col'))
The draws below stay inside these ranges and needn't reach their ends.
Inputs may be any that keep to these rules, and one draw needn't show every extreme that they name: rotated_slot is a permutation of all points; each point's rotated position lies on a device with the same col index; of the points of one device at most 1280 have rotated positions on any one device, and in every col group some device sends exactly 1280 to one device.
All inputs are finite; a program needn't handle non-finite values.
Results may differ from the reference program's by a relative error of at most 0.017.
Values may be sent and summed in bfloat16 or wider, within the bound.
A program may use at most 128 MiB of HBM per device.

```python
import math
import jax
import jax.numpy as jnp
from jax import lax

D = 256
HEADS = 8
FH = 1024
CW = 512
CHEADS = 8
CH = 2048
BALL = 256
PTS_DEV = 2048
POINTS = 65536
CBALL = 2048
CAP = 1280
N_ROW = 4
N_COL = 8


def draw_attend(key, model_width, leading):
    base = jnp.clip(jax.random.normal(key, (leading, model_width, 3, model_width), jnp.float32), -4.0, 4.0) / math.sqrt(model_width)
    query_part = base[:, :, 0]
    key_part = base[:, :, 1]
    value_part = base[:, :, 2]
    return jnp.concatenate((query_part, key_part, value_part), axis=-1)


def draw_fine_attend_in(key, part):
    return draw_attend(jax.random.fold_in(key, 11), D, 2).astype(jnp.bfloat16)


def draw_coarse_attend_in(key, part):
    return draw_attend(jax.random.fold_in(key, 13), CW, 1)[0].astype(jnp.bfloat16)


def draw_rotated_slot(key, part):
    key_order, key_shift, key_source, key_target = jax.random.split(jax.random.fold_in(key, 5), 4)
    orders = jax.vmap(lambda subkey: jax.random.permutation(subkey, N_ROW))(jax.random.split(key_order, N_COL))
    shifts = jax.random.randint(key_shift, (N_COL,), 1, N_ROW)
    source_rank = jax.vmap(lambda subkey: jnp.argsort(jax.random.permutation(subkey, PTS_DEV)))(jax.random.split(key_source, N_ROW * N_COL)).reshape(N_ROW, N_COL, PTS_DEV)
    target_spots = jax.vmap(lambda subkey: jax.random.permutation(subkey, PTS_DEV))(jax.random.split(key_target, N_ROW * N_COL)).reshape(N_ROW, N_COL, PTS_DEV)
    row_index = jnp.arange(N_ROW)[:, None]
    col_index = jnp.arange(N_COL)[None, :]
    first_target = orders[col_index, row_index]
    second = orders[col_index, (row_index + shifts[None, :]) % N_ROW]
    target = jnp.where(source_rank < CAP, first_target[:, :, None], second[:, :, None])
    local_spot = target_spots[target, col_index[:, :, None], source_rank]
    return ((target * N_COL + col_index[:, :, None]) * PTS_DEV + local_spot).reshape(-1).astype(jnp.int32)


def shard_levels(key, extent, shards, smallest, largest):
    def one(dim, parts):
        draws = jax.random.uniform(jax.random.fold_in(jax.random.fold_in(key, 6), dim), (parts,), jnp.float32, smallest / len(shards), largest / len(shards))
        return jnp.repeat(jnp.exp(draws), extent[dim] // parts).reshape((-1,) + (1,) * (len(extent) - dim - 1))

    gain = one(*shards[0])
    for cut in shards[1:]:
        gain = gain * one(*cut)
    return gain


def centred(rng, extent, scale, most, cuts=(), kind=jnp.bfloat16):
    drawn = scale * jax.random.normal(rng, extent, jnp.float32)
    if cuts:
        drawn = drawn * shard_levels(rng, extent, cuts, -0.22, 0.18)
    return jnp.clip(drawn, -most, most).astype(kind)


def setup_inputs(seed: int = 0) -> dict:
    key_list = jax.random.split(jax.random.key(seed), 13)
    return {
        "points": centred(key_list[0], (POINTS, D), 1.0, 6.0, ((0, 32),)),
        "rotated_slot": draw_rotated_slot(jax.random.fold_in(key_list[12], 71), 0),
        "fine_attend_in": draw_fine_attend_in(jax.random.fold_in(key_list[12], 71), 0),
        "fine_attend_out": centred(key_list[3], (2, D, D), D ** -0.5, 0.375),
        "fine_gate_up": centred(key_list[4], (2, D, 2 * FH), D ** -0.5, 0.375),
        "fine_down": centred(key_list[5], (2, FH, D), FH ** -0.5, 0.1875),
        "pool_weight": centred(key_list[6], (8 * D, CW), (8 * D) ** -0.5, 0.125),
        "coarse_attend_in": draw_coarse_attend_in(jax.random.fold_in(key_list[12], 71), 0),
        "coarse_attend_out": centred(key_list[8], (CW, CW), CW ** -0.5, 0.25),
        "coarse_gate_up": centred(key_list[9], (CW, 2 * CH), CW ** -0.5, 0.25),
        "coarse_down": centred(key_list[10], (CH, CW), CH ** -0.5, 0.125),
        "unpool_weight": centred(key_list[11], (CW, 8 * D), CW ** -0.5, 0.25),
    }


epsilon = 1e-06

def normed(source):
    widened = source.astype(jnp.float32)
    inverse_rms = lax.rsqrt(lax.optimization_barrier(jnp.mean(widened * widened, axis=-1, keepdims=True)) + epsilon)
    return (widened * inverse_rms).astype(jnp.bfloat16)

def ball_mix(queries, pairs, head_count):
    ball_count, query_len, model_width = queries.shape
    key_len = pairs.shape[1]
    head_size = model_width // head_count
    query_heads = queries.reshape(ball_count, query_len, head_count, head_size).astype(jnp.float32)
    key_heads = pairs[:, :, :model_width].reshape(ball_count, key_len, head_count, head_size).astype(jnp.float32)
    value_heads = pairs[:, :, model_width:].reshape(ball_count, key_len, head_count, head_size).astype(jnp.float32)
    scores = jnp.einsum('bqhd,bkhd->bhqk', query_heads, key_heads) * head_size ** (-0.5)
    row_max = lax.optimization_barrier(jnp.max(scores, axis=-1, keepdims=True))
    weights = jnp.exp(scores - row_max)
    weights = (weights / lax.optimization_barrier(jnp.sum(weights, axis=-1, keepdims=True))).astype(jnp.bfloat16)
    weights = lax.optimization_barrier(weights).astype(jnp.float32)
    mixture = jnp.einsum('bhqk,bkhd->bqhd', weights, value_heads)
    return mixture.reshape(ball_count, query_len, model_width).astype(jnp.bfloat16)

def attend(stream, attend_in, attend_out, head_count, ball_size):
    model_width = stream.shape[1]
    packed = jnp.dot(normed(stream), attend_in, preferred_element_type=jnp.float32).astype(jnp.bfloat16)
    queries = packed[:, :model_width].reshape(-1, ball_size, model_width)
    pairs = packed[:, model_width:].reshape(-1, ball_size, 2 * model_width)
    mixture = ball_mix(queries, pairs, head_count).reshape(-1, model_width)
    return jnp.dot(mixture, attend_out, preferred_element_type=jnp.float32)

def feed_forward(stream, gate_up, down_weight):
    both = jnp.dot(normed(stream), gate_up, preferred_element_type=jnp.float32)
    half_width = both.shape[1] // 2
    hidden = (jax.nn.silu(both[:, :half_width]) * both[:, half_width:]).astype(jnp.bfloat16)
    return (stream.astype(jnp.float32) + jnp.dot(hidden, down_weight, preferred_element_type=jnp.float32)).astype(jnp.bfloat16)

def blocked(function, source, block_size):
    pieces = source.reshape(-1, block_size, source.shape[-1])
    result = lax.map(function, pieces)
    return result.reshape(-1, result.shape[-1])

def reference(points, rotated_slot, fine_attend_in, fine_attend_out, fine_gate_up, fine_down, pool_weight, coarse_attend_in, coarse_attend_out, coarse_gate_up, coarse_down, unpool_weight):
    block_size = math.gcd(POINTS, 8192)

    def layer_one(stream):
        mixed = (stream.astype(jnp.float32) + attend(stream, fine_attend_in[0], fine_attend_out[0], HEADS, BALL)).astype(jnp.bfloat16)
        return feed_forward(mixed, fine_gate_up[0], fine_down[0])
    first = blocked(layer_one, points, block_size)
    rotated = jnp.zeros_like(first).at[rotated_slot].set(first)

    def turn(stream):
        return attend(stream, fine_attend_in[1], fine_attend_out[1], HEADS, BALL).astype(jnp.bfloat16)
    turned = blocked(turn, rotated, block_size)
    mixed_two = (first.astype(jnp.float32) + turned[rotated_slot].astype(jnp.float32)).astype(jnp.bfloat16)

    def layer_two(stream):
        return feed_forward(stream, fine_gate_up[1], fine_down[1])
    second = blocked(layer_two, mixed_two, block_size)
    pooled = jnp.dot(second.reshape(-1, 8 * D), pool_weight, preferred_element_type=jnp.float32).astype(jnp.bfloat16)

    def coarse_layer(stream):
        mixed = (stream.astype(jnp.float32) + attend(stream, coarse_attend_in, coarse_attend_out, CHEADS, CBALL)).astype(jnp.bfloat16)
        return feed_forward(mixed, coarse_gate_up, coarse_down)
    coarse = blocked(coarse_layer, pooled, CBALL)
    lifted = jnp.dot(normed(coarse), unpool_weight, preferred_element_type=jnp.float32).reshape(-1, D)
    return (second.astype(jnp.float32) + lifted).astype(jnp.bfloat16)
```

```python
import functools
import math

import jax
import jax.numpy as jnp
from jax import lax
from jax.experimental import pallas as pl
from jax.experimental.pallas import tpu as pltpu
from jax.sharding import PartitionSpec as P

HEADS = 8
CHEADS = 8
BALL = 256
GROUP = 8
FAN = 8
LANES = 128
EPS = 1e-06
F32 = jnp.float32
BF16 = jnp.bfloat16
LOG2E = 1.4426950408889634


def dot(a, b):
    return jnp.dot(a, b, preferred_element_type=F32)


def dot_t(a, b):
    return lax.dot_general(a, b, (((1,), (1,)), ((), ())), preferred_element_type=F32)


def normed(x):
    wide = x.astype(F32)
    return (wide * lax.rsqrt(jnp.mean(wide * wide, axis=-1, keepdims=True) + EPS)).astype(BF16)


def ff_sum(x, gate_up, down):
    both = dot(normed(x), gate_up)
    half = both.shape[1] // 2
    g = both[:, :half]
    hidden = ((0.5 * g) * (1.0 + jnp.tanh(0.5 * g)) * both[:, half:]).astype(BF16)
    return x.astype(F32) + dot(hidden, down)


def ball_mixture(packed):
    rows, width = packed.shape[0], packed.shape[1] // 3
    q, k, v = packed[:, :width], packed[:, width:2 * width], packed[:, 2 * width:]
    size = width // HEADS
    factor = size ** -0.5 * LOG2E
    half = width // 2
    head_of = lax.broadcasted_iota(jnp.int32, (rows, width), 1) // size
    zero = jnp.zeros((), BF16)
    parts = []
    for g in range(2):
        both = None
        for h in range(g * HEADS // 2, (g + 1) * HEADS // 2):
            mine = head_of == h
            s = dot_t(jnp.where(mine, q, zero), k)
            m = jnp.max(s, axis=-1, keepdims=True)
            e = jnp.exp2((s - m) * factor).astype(BF16)
            mine = mine[:, g * half:(g + 1) * half]
            value = jnp.concatenate(
                (
                    jnp.where(mine, v[:, g * half:(g + 1) * half], zero),
                    jnp.where(mine, jnp.ones((), BF16), zero),
                ),
                axis=1,
            )
            r = dot(e, value)
            both = r if both is None else both + r
        parts.append((both[:, :half] / both[:, half:]).astype(BF16))
    return jnp.concatenate(parts, axis=1)


def fine_attention(n, w_in, w_out):
    packed = dot(n, w_in).astype(BF16)
    balls = [ball_mixture(packed[i:i + BALL]) for i in range(0, n.shape[0], BALL)]
    return dot(jnp.concatenate(balls, axis=0), w_out)


def row_peers():
    me = lax.axis_index("row")
    near = me + 1 - 2 * (me % 2)
    far = me + 2 - 4 * ((me // 2) % 2)
    return me, near, far


def greet(peers, axis):
    barrier = pltpu.get_barrier_semaphore()
    for peer in peers:
        pl.semaphore_signal(
            barrier, inc=1, device_id={axis: peer}, device_id_type=pl.DeviceIdType.MESH
        )
    pl.semaphore_wait(barrier, len(peers))


PAIR = 2
RAW = 2
SENT = 4
COL_LAG = 3


class RowGather:
    def __init__(self, held, wide, send, recv):
        self.held, self.wide = held, wide
        self.send, self.recv = send, recv
        self.me, self.near, self.far = row_peers()
        self.last = self.far + self.near - self.me

    def copy(self, kind, c, block, peer):
        spot = self.held.at[block, pl.ds(c * BALL, BALL)]
        return self.between(kind, c, spot, spot, peer)

    def between(self, kind, c, source, target, peer):
        return pltpu.make_async_remote_copy(
            src_ref=source,
            dst_ref=target,
            send_sem=self.send.at[kind, c],
            recv_sem=self.recv.at[kind, c],
            device_id={"row": peer},
            device_id_type=pl.DeviceIdType.MESH,
        )

    def put(self, block, c, value):
        rows = self.held.shape[1]
        self.held[block, pl.ds(pl.multiple_of(c * BALL, BALL), BALL), :] = value
        self.widen(block, c, value)

    def widen(self, block, c, value):
        rows, width = self.held.shape[1:]
        parts = width // LANES
        at = pl.multiple_of((block * rows + c * BALL) * parts, BALL * parts)
        for t in range(parts):
            self.wide[pl.ds(at + t, BALL, stride=parts), :] = value[
                :, t * LANES:(t + 1) * LANES
            ].astype(F32)

    def arrived(self, block, c):
        at = pl.multiple_of(c * BALL, BALL)
        self.widen(block, c, self.held[block, pl.ds(at, BALL), :])

    def to_far(self, c):
        self.copy(0, c, self.me, self.far).start()

    def to_near(self, c):
        self.copy(1, c, self.me, self.near).start()

    def far_to_near(self, c):
        self.copy(2, c, self.far, self.near).start()

    def relay(self, c):
        self.copy(0, c, self.far, self.far).wait_recv()
        self.far_to_near(c)
        self.arrived(self.far, c)

    def from_near(self, c):
        self.copy(1, c, self.near, self.near).wait_recv()
        self.arrived(self.near, c)

    def from_last(self, c):
        self.copy(2, c, self.last, self.near).wait_recv()
        self.arrived(self.last, c)


def each(start, stop, do):
    def body(c, carry):
        do(c)
        return carry

    lax.fori_loop(start, stop, body, 0)


def positions(slot_all, target, col_size):
    lines, lanes = slot_all.shape[1:]
    rows = lines * lanes
    row_id = lax.broadcasted_iota(jnp.int32, (lines, lanes), 0)
    lane_id = lax.broadcasted_iota(jnp.int32, (lines, lanes), 1).astype(F32)
    sub_id = lax.broadcasted_iota(jnp.int32, (lanes, lanes), 0)
    left, right = [], []
    for r in range(slot_all.shape[0]):
        for c in range(lines):
            line = slot_all[r, c:c + 1, :]
            line = jnp.where(line // (rows * col_size) == target, line % rows, rows)
            hit = row_id == line // lanes
            left.append(
                jnp.concatenate(
                    (jnp.where(hit, float(r * lines + c), 0.0), jnp.where(hit, lane_id, 0.0)),
                    axis=0,
                ).astype(BF16)
            )
            right.append(jnp.where(sub_id == line % lanes, 1.0, 0.0).astype(BF16))
    found = dot_t(jnp.concatenate(left, axis=1), jnp.concatenate(right, axis=1))
    return (found[:lines] * lanes + found[lines:]).astype(jnp.int32)


def layer_one_kernel(
    col_size, points_hbm, slots_hbm, w_in_hbm, w_out_hbm, gate_up_hbm, down_hbm, out, wide,
    inverse, route, held, slot_all, points, w_in, w_out, gate_up, down, loaded, send, recv,
    s_send, s_recv,
):
    rows = out.shape[0]
    count = rows // BALL
    keep = count - RAW
    me, near, far = row_peers()
    other = far + near - me
    loads = [
        pltpu.make_async_copy(source, target, loaded.at[i])
        for i, (source, target) in enumerate(
            (
                (slots_hbm, slot_all.at[me]),
                (points_hbm, points.at[pl.ds(0, rows)]),
                (w_in_hbm.at[0], w_in),
                (w_out_hbm.at[0], w_out),
                (gate_up_hbm.at[0], gate_up),
                (down_hbm.at[0], down),
            )
        )
    ]
    for load in loads:
        load.start()
    greet((near, far, other), "row")
    gather = RowGather(held, wide, send, recv)

    def raw_copy(c):
        return gather.between(
            0,
            c,
            points.at[pl.ds(c * BALL, BALL)],
            points.at[pl.ds((c + RAW) * BALL, BALL)],
            far,
        )

    loads[1].wait()
    for c in range(keep, count):
        raw_copy(c).start()
    loads[0].wait()

    def slot_copy(kind, block, peer):
        return pltpu.make_async_remote_copy(
            src_ref=slot_all.at[me],
            dst_ref=slot_all.at[block],
            send_sem=s_send.at[kind],
            recv_sem=s_recv.at[kind],
            device_id={"row": peer},
            device_id_type=pl.DeviceIdType.MESH,
        )

    for kind, peer in enumerate((near, far, other)):
        slot_copy(kind, me, peer).start()
    slots = slot_all[me]
    parts = out.shape[1] // LANES
    route[...] = (slots // (rows * col_size) * rows + slots % rows) * parts
    for load in loads[2:]:
        load.wait()

    own_steps = count // PAIR
    sent_steps = keep // PAIR
    span = PAIR * BALL

    def step(s, carry):
        @pl.when(s == own_steps)
        def _():
            for c in range(keep, count):
                raw_copy(c).wait_recv()

        u = points[pl.ds(pl.multiple_of(s * span, span), span), :]
        mixed = (u.astype(F32) + fine_attention(normed(u), w_in[...], w_out[...])).astype(BF16)
        value = ff_sum(mixed, gate_up[...], down[...]).astype(BF16)

        @pl.when(s < own_steps)
        def _():
            out[pl.ds(pl.multiple_of(s * span, span), span), :] = value

        unit = normed(value)
        again = s // own_steps
        block = me + (far - me) * again
        first = s * PAIR - RAW * again
        for i in range(PAIR):
            gather.put(block, first + i, unit[i * BALL:(i + 1) * BALL])

            @pl.when(s < sent_steps)
            def _():
                gather.to_far(first + i)

            @pl.when(s < own_steps)
            def _():
                gather.to_near(first + i)

            @pl.when(s == own_steps)
            def _():
                gather.far_to_near(first + i)

        @pl.when(s >= 1)
        def _():
            for i in range(PAIR):
                gather.from_near((s - 1) * PAIR + i)

        @pl.when(s >= 2)
        def _():
            gather.relay(s - 2)

        return carry

    lax.fori_loop(0, own_steps + 1, step, 0)
    done = own_steps - 1
    for kind, peer in enumerate((near, far, other)):
        slot_copy(kind, peer, peer).wait()
    lines = slot_all.shape[1]
    inverse[:lines] = positions(slot_all, me, col_size) * parts
    inverse[lines:] = positions(slot_all, far, col_size) * parts
    each(keep, count, gather.from_last)
    each(0, done - 1, gather.from_last)

    def tail(c):
        gather.relay(c)
        gather.from_last(c - 1)

    each(done, keep, tail)
    gather.from_last(keep - 1)

    def end(c):
        gather.copy(1, c, me, near).wait_send()
        gather.copy(2, c, far, near).wait_send()

    each(0, count, end)
    each(0, keep, lambda c: gather.copy(0, c, me, far).wait_send())
    for c in range(keep, count):
        raw_copy(c).wait_send()


def take_rows(wide, index, base, taken):
    parts = taken.shape[0] // BALL
    for i in range(BALL):
        taken[pl.ds(i * parts, parts), :] = wide[pl.ds(index[base + i], parts), :]


def taken_rows(taken):
    parts = taken.shape[0] // BALL
    return jnp.concatenate(
        [taken[pl.ds(t, BALL, stride=parts), :] for t in range(parts)], axis=1
    )


def turn_kernel(source, index, w_in, w_out, wide, held, taken, send, recv):
    rows = held.shape[1]
    count = rows // BALL
    steps = (2 * count - SENT) // PAIR
    own_steps = count // PAIR
    sent_steps = SENT // PAIR
    me, near, far = row_peers()
    greet((near, far), "row")
    gather = RowGather(held, wide, send, recv)

    def base_of(n):
        return (n + SENT * (n // count)) * BALL

    def fetch(s):
        for i in range(PAIR):
            take_rows(source, index, base_of(s * PAIR + i), taken.at[i])

    fetch(0)

    def step(s, carry):
        u = jnp.concatenate([taken_rows(taken.at[i]) for i in range(PAIR)], axis=0).astype(BF16)
        fetch(jnp.minimum(s + 1, steps - 1))
        value = fine_attention(u, w_in[1], w_out[1]).astype(BF16)
        again = s // own_steps
        block = me + (far - me) * again
        first = s * PAIR + (SENT - count) * again
        for i in range(PAIR):
            gather.put(block, first + i, value[i * BALL:(i + 1) * BALL])

            @pl.when(s < sent_steps)
            def _():
                gather.to_far(first + i)

            @pl.when(s < own_steps)
            def _():
                gather.to_near(first + i)

            @pl.when(s >= own_steps)
            def _():
                gather.far_to_near(first + i)

        @pl.when((s >= 1) & (s <= own_steps))
        def _():
            for i in range(PAIR):
                gather.from_near((s - 1) * PAIR + i)

        @pl.when((s >= 3) & (s < SENT + 3))
        def _():
            gather.relay(s - 3)

        @pl.when(s > own_steps)
        def _():
            for i in range(PAIR):
                gather.from_last((s - 1) * PAIR + SENT - count + i)

        return carry

    lax.fori_loop(0, steps, step, 0)
    done = min(max(steps - 3, 0), SENT)
    each((steps - 1) * PAIR + SENT - count, count, gather.from_last)
    each(done, SENT, gather.relay)
    each(0, SENT, gather.from_last)

    def end(c):
        gather.copy(1, c, me, near).wait_send()
        gather.copy(2, c, far, near).wait_send()

    each(0, count, end)
    each(0, SENT, lambda c: gather.copy(0, c, me, far).wait_send())


def layer_two_kernel(
    first, wide, index, gate_up, down, pool, w_in, second, own, queries, keys, values, pooled,
    taken, tall, send, recv
):
    rows = second.shape[0]
    count = rows // BALL
    small = BALL // FAN
    col = lax.axis_index("col")
    me = col % GROUP
    base = col - me
    flip = me + 1 - 2 * (me % 2)
    peers = [(me + 2 * step) % GROUP for step in range(1, GROUP // 2)]
    greet([base + p for p in [flip] + peers], "col")
    pieces = recv.shape[1]
    piece = pooled.shape[1] // pieces
    per = count // pieces

    def copy(kind, c, block, peer):
        spot = pooled.at[block, pl.ds(c * piece, piece)]
        return pltpu.make_async_remote_copy(
            src_ref=spot,
            dst_ref=spot,
            send_sem=send.at[kind, c],
            recv_sem=recv.at[kind, c],
            device_id={"col": base + peer},
            device_id_type=pl.DeviceIdType.MESH,
        )

    lead = GROUP // 2

    def source_of(kind):
        return (me + GROUP - 2 * kind) % GROUP

    def step(c, carry):
        def ball(i, carry):
            b = c * per + i
            at = pl.multiple_of(b * BALL, BALL)
            take_rows(wide, index, b * BALL, taken)
            mixed = (first[pl.ds(at, BALL), :].astype(F32) + taken_rows(taken)).astype(BF16)
            result = ff_sum(mixed, gate_up[1], down[1]).astype(BF16)
            second[pl.ds(at, BALL), :] = result
            for t in range(tall.shape[0]):
                tall[t, pl.ds(pl.multiple_of(i * BALL, BALL), BALL), :] = result[
                    :, t * LANES:(t + 1) * LANES
                ].astype(F32)
            return carry

        lax.fori_loop(0, per, ball, 0)
        side = [
            tall[t, pl.ds(j, piece, stride=FAN), :].astype(BF16)
            for j in range(FAN)
            for t in range(tall.shape[0])
        ]
        total = dot(jnp.concatenate(side, axis=1), pool[...])
        pooled[me, pl.ds(pl.multiple_of(c * piece, piece), piece), :] = total.astype(BF16)
        copy(0, c, me, flip).start()
        for kind in range(1, lead):
            copy(kind, c, me, peers[kind - 1]).start()

        @pl.when(c >= COL_LAG)
        def _():
            relay(c - COL_LAG, 0)

        return carry

    def relay(c, carry):
        for kind in range(1, lead):
            copy(kind, c, source_of(kind), peers[0]).wait_recv()
            copy(lead - 1 + kind, c, source_of(kind), flip).start()
        return carry

    lax.fori_loop(0, pieces, step, 0)
    width = pool.shape[1]
    block_rows = pooled.shape[1]
    half = block_rows // 2

    def project(block, at, size):
        packed = dot(normed(pooled[block, at:at + size, :]), w_in[:, width:]).astype(BF16)
        spot = pl.ds(pl.multiple_of(block * block_rows + at, size), size)
        keys[spot, :] = packed[:, :width]
        values[spot, :] = packed[:, width:]

    def arrived(kind, block):
        def one(c, carry):
            copy(kind, c, block, flip).wait_recv()
            return carry

        lax.fori_loop(0, pieces, one, 0)

    direct = [source_of(kind) for kind in range(1, lead)]
    own[...] = pooled[me]
    queries[...] = dot(normed(pooled[me]), w_in[:, :width]).astype(BF16)
    project(me, 0, block_rows)
    start = max(pieces - COL_LAG, 0)
    for c in range(start, pieces):
        relay(c, 0)
        if c == start:
            arrived(0, flip)
            project(flip, 0, block_rows)
        if c == start + 1:
            for block in direct:
                project(block, 0, half)
    for block in direct:
        project(block, half, half)
    for kind in range(1, lead):
        origin = source_of(kind)
        block = origin + 1 - 2 * (origin % 2)
        arrived(lead - 1 + kind, block)
        project(block, 0, block_rows)

    def end(c, carry):
        copy(0, c, me, flip).wait_send()
        for kind in range(1, lead):
            copy(kind, c, me, peers[kind - 1]).wait_send()
            copy(lead - 1 + kind, c, source_of(kind), flip).wait_send()
        return carry

    lax.fori_loop(0, pieces, end, 0)


def coarse_kernel(
    pooled, queries, keys, values, second, w_out, gate_up, down, unpool, out, lifted
):
    own = pooled[...]
    rows, width = own.shape
    size = width // CHEADS
    factor = size ** -0.5 * LOG2E
    q = queries[...]
    part = 256
    head_of = lax.broadcasted_iota(jnp.int32, (rows, part), 1) // size
    zero = jnp.zeros((), BF16)
    mixture = []
    for g in range(width // part):
        at = g * part
        acc = jnp.zeros((rows, part), F32)
        for h in range(part // size):
            mine = head_of == h
            s = dot_t(jnp.where(mine, q[:, at:at + part], zero), keys[:, at:at + part])
            m = jnp.max(s, axis=-1, keepdims=True)
            e = jnp.exp2((s - m) * factor)
            r = dot(e.astype(BF16), values[:, at:at + part])
            acc = jnp.where(mine, r / jnp.sum(e, axis=-1, keepdims=True), acc)
        mixture.append(acc.astype(BF16))
    mixed = (own.astype(F32) + dot(jnp.concatenate(mixture, axis=1), w_out[...])).astype(BF16)
    coarse = ff_sum(mixed, gate_up[...], down[...]).astype(BF16)
    up = normed(coarse)
    fine = out.shape[1]
    for j in range(FAN):
        part_up = dot(up, unpool[:, j * fine:(j + 1) * fine])
        for t in range(lifted.shape[0]):
            lifted[t, pl.ds(j, rows, stride=FAN), :] = part_up[:, t * LANES:(t + 1) * LANES]
    for c in range(out.shape[0] // BALL):
        at = c * BALL
        for t in range(lifted.shape[0]):
            lane = slice(t * LANES, (t + 1) * LANES)
            out[at:at + BALL, lane] = (
                second[at:at + BALL, lane].astype(F32) + lifted[t, at:at + BALL, :]
            ).astype(BF16)


VMEM = pl.BlockSpec(memory_space=pltpu.VMEM)
SMEM = pl.BlockSpec(memory_space=pltpu.SMEM)
DMA = pltpu.SemaphoreType.DMA


def local(
    points,
    rotated_slot,
    fine_attend_in,
    fine_attend_out,
    fine_gate_up,
    fine_down,
    pool_weight,
    coarse_attend_in,
    coarse_attend_out,
    coarse_gate_up,
    coarse_down,
    unpool_weight,
):
    rows, width = points.shape
    row_size = lax.axis_size("row")
    col_size = lax.axis_size("col")
    count = rows // BALL
    small = rows // FAN
    coarse_width = pool_weight.shape[1]
    lanes = LANES
    lines = rows // lanes
    mib = 1024 * 1024
    parts = width // LANES
    everyone = jax.ShapeDtypeStruct((row_size * rows * parts, LANES), F32)
    gathered = pltpu.VMEM((BALL * parts, LANES), F32)
    held = pltpu.VMEM((row_size, rows, width), BF16)
    scalars = jax.ShapeDtypeStruct((lines, lanes), jnp.int32)
    both = jax.ShapeDtypeStruct((2 * lines, lanes), jnp.int32)

    first, wide, inverse, route = pl.pallas_call(
        functools.partial(layer_one_kernel, col_size),
        out_shape=(jax.ShapeDtypeStruct((rows, width), BF16), everyone, both, scalars),
        in_specs=[pl.BlockSpec(memory_space=pltpu.HBM)] * 6,
        out_specs=(VMEM,) * 4,
        scratch_shapes=[
            held,
            pltpu.VMEM((row_size, lines, lanes), jnp.int32),
            pltpu.VMEM((rows + RAW * BALL, width), BF16),
            pltpu.VMEM(fine_attend_in.shape[1:], BF16),
            pltpu.VMEM(fine_attend_out.shape[1:], BF16),
            pltpu.VMEM(fine_gate_up.shape[1:], BF16),
            pltpu.VMEM(fine_down.shape[1:], BF16),
            DMA((6,)),
            DMA((3, count)),
            DMA((3, count)),
            DMA((3,)),
            DMA((3,)),
        ],
        compiler_params=pltpu.CompilerParams(
            collective_id=0, has_side_effects=True, vmem_limit_bytes=36 * mib
        ),
        name="layer_one",
    )(
        *(
            pltpu.with_memory_space_constraint(array, pltpu.HBM)
            for array in (
                points,
                rotated_slot.reshape(lines, lanes),
                fine_attend_in,
                fine_attend_out,
                fine_gate_up,
                fine_down,
            )
        )
    )

    turned = pl.pallas_call(
        turn_kernel,
        out_shape=everyone,
        in_specs=[VMEM, SMEM, VMEM, VMEM],
        out_specs=VMEM,
        scratch_shapes=[
            held,
            pltpu.VMEM((PAIR, BALL * parts, LANES), F32),
            DMA((3, count)),
            DMA((3, count)),
        ],
        compiler_params=pltpu.CompilerParams(
            collective_id=1, has_side_effects=True, vmem_limit_bytes=24 * mib
        ),
        name="turn",
    )(wide, inverse.reshape(-1), fine_attend_in, fine_attend_out)

    pieces = count
    kinds = GROUP - 1
    one = jax.ShapeDtypeStruct((small, coarse_width), BF16)
    every = jax.ShapeDtypeStruct((GROUP * small, coarse_width), BF16)
    second, *coarse_parts = pl.pallas_call(
        layer_two_kernel,
        out_shape=(
            jax.ShapeDtypeStruct((rows, width), BF16),
            one,
            one,
            every,
            every,
        ),
        in_specs=[VMEM, VMEM, SMEM, VMEM, VMEM, VMEM, VMEM],
        out_specs=(VMEM,) * 5,
        scratch_shapes=[
            pltpu.VMEM((GROUP, small, coarse_width), BF16),
            gathered,
            pltpu.VMEM((width // LANES, rows // pieces, LANES), F32),
            DMA((kinds, pieces)),
            DMA((kinds, pieces)),
        ],
        compiler_params=pltpu.CompilerParams(
            collective_id=2, has_side_effects=True, vmem_limit_bytes=20 * mib
        ),
        name="layer_two",
    )(first, turned, route.reshape(-1), fine_gate_up, fine_down, pool_weight, coarse_attend_in)

    return pl.pallas_call(
        coarse_kernel,
        out_shape=jax.ShapeDtypeStruct((rows, width), BF16),
        in_specs=[VMEM] * 9,
        out_specs=VMEM,
        scratch_shapes=[
            pltpu.VMEM((width // LANES, rows, LANES), F32),
        ],
        compiler_params=pltpu.CompilerParams(vmem_limit_bytes=22 * mib),
        name="coarse",
    )(
        *coarse_parts,
        second,
        coarse_attend_out,
        coarse_gate_up,
        coarse_down,
        unpool_weight,
    )


def solution(mesh):
    split = P(("row", "col"), None)
    placed = (split, P(("row", "col"))) + (P(),) * 10
    return jax.shard_map(local, mesh=mesh, in_specs=placed, out_specs=split, check_vma=False)
```

```python
import functools
import math

import jax
import jax.numpy as jnp
from jax import lax
from jax.experimental import pallas as pl
from jax.experimental.pallas import tpu as pltpu
from jax.sharding import PartitionSpec as P

HEADS = 8
CHEADS = 8
BALL = 256
GROUP = 8
FAN = 8
LANES = 128
EPS = 1e-06
F32 = jnp.float32
BF16 = jnp.bfloat16
LOG2E = 1.4426950408889634


def dot(a, b):
    return jnp.dot(a, b, preferred_element_type=F32)


def dot_t(a, b):
    return lax.dot_general(a, b, (((1,), (1,)), ((), ())), preferred_element_type=F32)


def normed(x):
    wide = x.astype(F32)
    return (wide * lax.rsqrt(jnp.mean(wide * wide, axis=-1, keepdims=True) + EPS)).astype(BF16)


def ff_sum(x, gate_up, down):
    both = dot(normed(x), gate_up)
    half = both.shape[1] // 2
    g = both[:, :half]
    hidden = ((0.5 * g) * (1.0 + jnp.tanh(0.5 * g)) * both[:, half:]).astype(BF16)
    return x.astype(F32) + dot(hidden, down)


def ball_mixture(packed):
    rows, width = packed.shape[0], packed.shape[1] // 3
    q, k, v = packed[:, :width], packed[:, width:2 * width], packed[:, 2 * width:]
    size = width // HEADS
    factor = size ** -0.5 * LOG2E
    half = width // 2
    head_of = lax.broadcasted_iota(jnp.int32, (rows, width), 1) // size
    zero = jnp.zeros((), BF16)
    parts = []
    for g in range(2):
        both = None
        for h in range(g * HEADS // 2, (g + 1) * HEADS // 2):
            mine = head_of == h
            s = dot_t(jnp.where(mine, q, zero), k)
            m = jnp.max(s, axis=-1, keepdims=True)
            e = jnp.exp2((s - m) * factor).astype(BF16)
            mine = mine[:, g * half:(g + 1) * half]
            value = jnp.concatenate(
                (
                    jnp.where(mine, v[:, g * half:(g + 1) * half], zero),
                    jnp.where(mine, jnp.ones((), BF16), zero),
                ),
                axis=1,
            )
            r = dot(e, value)
            both = r if both is None else both + r
        parts.append((both[:, :half] / both[:, half:]).astype(BF16))
    return jnp.concatenate(parts, axis=1)


def fine_attention(n, w_in, w_out):
    packed = dot(n, w_in).astype(BF16)
    balls = [ball_mixture(packed[i:i + BALL]) for i in range(0, n.shape[0], BALL)]
    return dot(jnp.concatenate(balls, axis=0), w_out)


def row_peers():
    me = lax.axis_index("row")
    near = me + 1 - 2 * (me % 2)
    far = me + 2 - 4 * ((me // 2) % 2)
    return me, near, far


def greet(peers, axis):
    barrier = pltpu.get_barrier_semaphore()
    for peer in peers:
        pl.semaphore_signal(
            barrier, inc=1, device_id={axis: peer}, device_id_type=pl.DeviceIdType.MESH
        )
    pl.semaphore_wait(barrier, len(peers))


PAIR = 2
RAW = 2
SENT = 4


class RowGather:
    def __init__(self, held, wide, send, recv):
        self.held, self.wide = held, wide
        self.send, self.recv = send, recv
        self.me, self.near, self.far = row_peers()
        self.last = self.far + self.near - self.me

    def copy(self, kind, c, block, peer):
        spot = self.held.at[block, pl.ds(c * BALL, BALL)]
        return self.between(kind, c, spot, spot, peer)

    def between(self, kind, c, source, target, peer):
        return pltpu.make_async_remote_copy(
            src_ref=source,
            dst_ref=target,
            send_sem=self.send.at[kind, c],
            recv_sem=self.recv.at[kind, c],
            device_id={"row": peer},
            device_id_type=pl.DeviceIdType.MESH,
        )

    def put(self, block, c, value):
        rows = self.held.shape[1]
        self.held[block, pl.ds(pl.multiple_of(c * BALL, BALL), BALL), :] = value
        self.widen(block, c, value)

    def widen(self, block, c, value):
        rows, width = self.held.shape[1:]
        parts = width // LANES
        at = pl.multiple_of((block * rows + c * BALL) * parts, BALL * parts)
        for t in range(parts):
            self.wide[pl.ds(at + t, BALL, stride=parts), :] = value[
                :, t * LANES:(t + 1) * LANES
            ].astype(F32)

    def arrived(self, block, c):
        at = pl.multiple_of(c * BALL, BALL)
        self.widen(block, c, self.held[block, pl.ds(at, BALL), :])

    def to_far(self, c):
        self.copy(0, c, self.me, self.far).start()

    def to_near(self, c):
        self.copy(1, c, self.me, self.near).start()

    def far_to_near(self, c):
        self.copy(2, c, self.far, self.near).start()

    def relay(self, c):
        self.copy(0, c, self.far, self.far).wait_recv()
        self.far_to_near(c)
        self.arrived(self.far, c)

    def from_near(self, c):
        self.copy(1, c, self.near, self.near).wait_recv()
        self.arrived(self.near, c)

    def from_last(self, c):
        self.copy(2, c, self.last, self.near).wait_recv()
        self.arrived(self.last, c)


def each(start, stop, do):
    def body(c, carry):
        do(c)
        return carry

    lax.fori_loop(start, stop, body, 0)


def positions(slot_all, target, col_size):
    lines, lanes = slot_all.shape[1:]
    rows = lines * lanes
    row_id = lax.broadcasted_iota(jnp.int32, (lines, lanes), 0)
    lane_id = lax.broadcasted_iota(jnp.int32, (lines, lanes), 1).astype(F32)
    sub_id = lax.broadcasted_iota(jnp.int32, (lanes, lanes), 0)
    left, right = [], []
    for r in range(slot_all.shape[0]):
        for c in range(lines):
            line = slot_all[r, c:c + 1, :]
            line = jnp.where(line // (rows * col_size) == target, line % rows, rows)
            hit = row_id == line // lanes
            left.append(
                jnp.concatenate(
                    (jnp.where(hit, float(r * lines + c), 0.0), jnp.where(hit, lane_id, 0.0)),
                    axis=0,
                ).astype(BF16)
            )
            right.append(jnp.where(sub_id == line % lanes, 1.0, 0.0).astype(BF16))
    found = dot_t(jnp.concatenate(left, axis=1), jnp.concatenate(right, axis=1))
    return (found[:lines] * lanes + found[lines:]).astype(jnp.int32)


def layer_one_kernel(
    col_size, points_hbm, slots_hbm, w_in_hbm, w_out_hbm, gate_up_hbm, down_hbm, out, wide,
    inverse, route, held, slot_all, points, w_in, w_out, gate_up, down, loaded, send, recv,
    s_send, s_recv,
):
    rows = out.shape[0]
    count = rows // BALL
    keep = count - RAW
    me, near, far = row_peers()
    other = far + near - me
    loads = [
        pltpu.make_async_copy(source, target, loaded.at[i])
        for i, (source, target) in enumerate(
            (
                (slots_hbm, slot_all.at[me]),
                (points_hbm, points.at[pl.ds(0, rows)]),
                (w_in_hbm.at[0], w_in),
                (w_out_hbm.at[0], w_out),
                (gate_up_hbm.at[0], gate_up),
                (down_hbm.at[0], down),
            )
        )
    ]
    for load in loads:
        load.start()
    greet((near, far, other), "row")
    gather = RowGather(held, wide, send, recv)

    def raw_copy(c):
        return gather.between(
            0,
            c,
            points.at[pl.ds(c * BALL, BALL)],
            points.at[pl.ds((c + RAW) * BALL, BALL)],
            far,
        )

    loads[1].wait()
    for c in range(keep, count):
        raw_copy(c).start()
    loads[0].wait()

    def slot_copy(kind, block, peer):
        return pltpu.make_async_remote_copy(
            src_ref=slot_all.at[me],
            dst_ref=slot_all.at[block],
            send_sem=s_send.at[kind],
            recv_sem=s_recv.at[kind],
            device_id={"row": peer},
            device_id_type=pl.DeviceIdType.MESH,
        )

    for kind, peer in enumerate((near, far, other)):
        slot_copy(kind, me, peer).start()
    slots = slot_all[me]
    parts = out.shape[1] // LANES
    route[...] = (slots // (rows * col_size) * rows + slots % rows) * parts
    for load in loads[2:]:
        load.wait()

    own_steps = count // PAIR
    sent_steps = keep // PAIR
    span = PAIR * BALL

    def step(s, carry):
        @pl.when(s == own_steps)
        def _():
            for c in range(keep, count):
                raw_copy(c).wait_recv()

        u = points[pl.ds(pl.multiple_of(s * span, span), span), :]
        mixed = (u.astype(F32) + fine_attention(normed(u), w_in[...], w_out[...])).astype(BF16)
        value = ff_sum(mixed, gate_up[...], down[...]).astype(BF16)

        @pl.when(s < own_steps)
        def _():
            out[pl.ds(pl.multiple_of(s * span, span), span), :] = value

        unit = normed(value)
        again = s // own_steps
        block = me + (far - me) * again
        first = s * PAIR - RAW * again
        for i in range(PAIR):
            gather.put(block, first + i, unit[i * BALL:(i + 1) * BALL])

            @pl.when(s < sent_steps)
            def _():
                gather.to_far(first + i)

            @pl.when(s < own_steps)
            def _():
                gather.to_near(first + i)

            @pl.when(s == own_steps)
            def _():
                gather.far_to_near(first + i)

        @pl.when(s >= 1)
        def _():
            for i in range(PAIR):
                gather.from_near((s - 1) * PAIR + i)

        @pl.when(s >= 2)
        def _():
            gather.relay(s - 2)

        return carry

    lax.fori_loop(0, own_steps + 1, step, 0)
    done = own_steps - 1
    for kind, peer in enumerate((near, far, other)):
        slot_copy(kind, peer, peer).wait()
    lines = slot_all.shape[1]
    inverse[:lines] = positions(slot_all, me, col_size) * parts
    inverse[lines:] = positions(slot_all, far, col_size) * parts
    each(keep, count, gather.from_last)
    each(0, done - 1, gather.from_last)

    def tail(c):
        gather.relay(c)
        gather.from_last(c - 1)

    each(done, keep, tail)
    gather.from_last(keep - 1)

    def end(c):
        gather.copy(1, c, me, near).wait_send()
        gather.copy(2, c, far, near).wait_send()

    each(0, count, end)
    each(0, keep, lambda c: gather.copy(0, c, me, far).wait_send())
    for c in range(keep, count):
        raw_copy(c).wait_send()


def take_rows(wide, index, base, taken):
    parts = taken.shape[0] // BALL
    for i in range(BALL):
        taken[pl.ds(i * parts, parts), :] = wide[pl.ds(index[base + i], parts), :]


def taken_rows(taken):
    parts = taken.shape[0] // BALL
    return jnp.concatenate(
        [taken[pl.ds(t, BALL, stride=parts), :] for t in range(parts)], axis=1
    )


def turn_kernel(source, index, w_in, w_out, wide, held, taken, send, recv):
    rows = held.shape[1]
    count = rows // BALL
    steps = (2 * count - SENT) // PAIR
    own_steps = count // PAIR
    sent_steps = SENT // PAIR
    me, near, far = row_peers()
    greet((near, far), "row")
    gather = RowGather(held, wide, send, recv)

    def base_of(n):
        return (n + SENT * (n // count)) * BALL

    def fetch(s):
        for i in range(PAIR):
            take_rows(source, index, base_of(s * PAIR + i), taken.at[i])

    fetch(0)

    def step(s, carry):
        u = jnp.concatenate([taken_rows(taken.at[i]) for i in range(PAIR)], axis=0).astype(BF16)
        fetch(jnp.minimum(s + 1, steps - 1))
        value = fine_attention(u, w_in[1], w_out[1]).astype(BF16)
        again = s // own_steps
        block = me + (far - me) * again
        first = s * PAIR + (SENT - count) * again
        for i in range(PAIR):
            gather.put(block, first + i, value[i * BALL:(i + 1) * BALL])

            @pl.when(s < sent_steps)
            def _():
                gather.to_far(first + i)

            @pl.when(s < own_steps)
            def _():
                gather.to_near(first + i)

            @pl.when(s >= own_steps)
            def _():
                gather.far_to_near(first + i)

        @pl.when((s >= 1) & (s <= own_steps))
        def _():
            for i in range(PAIR):
                gather.from_near((s - 1) * PAIR + i)

        @pl.when((s >= 3) & (s < SENT + 3))
        def _():
            gather.relay(s - 3)

        @pl.when(s > own_steps)
        def _():
            for i in range(PAIR):
                gather.from_last((s - 1) * PAIR + SENT - count + i)

        return carry

    lax.fori_loop(0, steps, step, 0)
    done = min(max(steps - 3, 0), SENT)
    each((steps - 1) * PAIR + SENT - count, count, gather.from_last)
    each(done, SENT, gather.relay)
    each(0, SENT, gather.from_last)

    def end(c):
        gather.copy(1, c, me, near).wait_send()
        gather.copy(2, c, far, near).wait_send()

    each(0, count, end)
    each(0, SENT, lambda c: gather.copy(0, c, me, far).wait_send())


class ColGather:
    def __init__(self, pooled, send, recv):
        self.pooled, self.send, self.recv = pooled, send, recv
        self.pieces = recv.shape[1]
        self.half = self.pieces // 2
        self.piece = pooled.shape[1] // self.pieces
        col = lax.axis_index("col")
        me = col % GROUP
        self.me, self.base = me, col - me
        side, line = me % 2, me // 2
        self.over = 1 - 2 * side
        self.flip = me + self.over
        self.pair = me + 2 - 4 * (line % 2)
        self.across = (GROUP // 2 - 1 - line) * 2 + side
        self.second = side + 4 - 2 * (line // 2)
        self.third = side + 6 - 6 * (line // 2)
        self.inner = (line == 1) | (line == 2)
        self.outer = (line == 0) | (line == 3)

    def copy(self, kind, c, block, peer):
        spot = self.pooled.at[block, pl.ds(c * self.piece, self.piece)]
        return pltpu.make_async_remote_copy(
            src_ref=spot,
            dst_ref=spot,
            send_sem=self.send.at[kind, c],
            recv_sem=self.recv.at[block, c],
            device_id={"col": self.base + peer},
            device_id_type=pl.DeviceIdType.MESH,
        )

    def moves(self, kind):
        return (
            (self.me, self.pair),
            (self.me, self.flip),
            (self.me, self.across),
            (self.pair, self.across),
            (self.second, self.pair),
            (self.third, self.pair),
            (self.pair, self.flip),
            (self.second, self.flip),
            (self.third, self.flip),
            (self.flip, self.pair),
        )[kind]

    def go(self, kind, c):
        self.copy(kind, c, *self.moves(kind)).start()

    def landed(self, block, c):
        self.copy(0, c, block, self.pair).wait_recv()

    def all_landed(self, block):
        each(0, self.pieces, lambda c: self.landed(block, c))

    def own(self, c):
        self.go(0, c)
        self.go(1, c)

        @pl.when(self.inner)
        def _():
            self.go(2, c)

    def pass_pair(self, c):
        self.landed(self.pair, c)

        @pl.when(self.inner)
        def _():
            self.go(3, c)

        @pl.when(c < self.half)
        def _():
            self.go(6, c)

    def pass_second(self, c):
        self.landed(self.second, c)

        @pl.when(self.inner)
        def _():
            self.go(4, c)

        self.go(7, c)

    def pass_third(self, c):
        self.landed(self.third, c)

        @pl.when(self.inner)
        def _():
            self.go(5, c)

        self.go(8, c)

    def pass_flip(self):
        each(self.half, self.pieces, lambda c: self.go(9, c))

    def block_of(self, i):
        order = (
            self.me,
            self.flip,
            self.pair,
            self.second,
            self.second + self.over,
            self.third,
            self.pair + self.over,
            self.third + self.over,
        )
        block = order[0]
        for at in range(1, GROUP):
            block = block + (order[at] - order[at - 1]) * ((i + GROUP - at) // GROUP)
        return block

    def before(self, i):
        last = self.pieces - 1

        @pl.when(i == 1)
        def _():
            self.pass_pair(last)

        @pl.when((i == 1) & self.inner)
        def _():
            self.pass_second(last)
            self.pass_third(1)

        @pl.when((i == 1) & self.outer)
        def _():
            self.pass_second(1)

        @pl.when(i == 1)
        def _():
            self.all_landed(self.flip)

        @pl.when((i == 1) & self.outer)
        def _():
            self.pass_flip()

        @pl.when((i == 2) & self.inner)
        def _():
            self.pass_third(2)

        @pl.when((i == 3) & self.inner)
        def _():
            each(3, self.pieces, self.pass_third)
            self.pass_flip()

        @pl.when((i == 3) & self.outer)
        def _():
            each(2, self.pieces, self.pass_second)

        @pl.when((i == 4) & self.outer)
        def _():
            each(0, 2, self.pass_third)

        @pl.when(i == 4)
        def _():
            self.all_landed(self.second + self.over)

        @pl.when((i == 5) & self.outer)
        def _():
            each(2, self.pieces, self.pass_third)

        @pl.when(i == 6)
        def _():
            self.all_landed(self.pair + self.over)

        @pl.when(i == 7)
        def _():
            self.all_landed(self.third + self.over)

    def during(self, c):
        @pl.when(c >= 1)
        def _():
            self.pass_pair(c - 1)

        @pl.when((c >= 1) & self.inner)
        def _():
            self.pass_second(c - 1)

        @pl.when((c == self.pieces - 1) & self.inner)
        def _():
            self.pass_third(0)

        @pl.when((c == self.pieces - 1) & self.outer)
        def _():
            self.pass_second(0)

    def finish(self):
        def sent(kind):
            return lambda c: self.copy(kind, c, *self.moves(kind)).wait_send()

        for kind in (0, 1, 7, 8):
            each(0, self.pieces, sent(kind))
        each(0, self.half, sent(6))
        each(self.half, self.pieces, sent(9))

        @pl.when(self.inner)
        def _():
            for kind in (2, 3, 4, 5):
                each(0, self.pieces, sent(kind))


def layer_two_kernel(
    first, wide, index, gate_up, down, pool, w_in, second, own, mixture, pooled, taken, tall,
    queries, top, value_sum, weight_sum, send, recv
):
    rows = second.shape[0]
    span = PAIR * BALL
    gather = ColGather(pooled, send, recv)
    me, pieces, piece = gather.me, gather.pieces, gather.piece
    greet([gather.base + p for p in (gather.flip, gather.pair, gather.across)], "col")

    def fetch(c):
        for i in range(PAIR):
            take_rows(wide, index, (c * PAIR + i) * BALL, taken.at[i])

    fetch(0)

    def step(c, carry):
        at = pl.multiple_of(c * span, span)
        turned = jnp.concatenate([taken_rows(taken.at[i]) for i in range(PAIR)], axis=0)
        mixed = (first[pl.ds(at, span), :].astype(F32) + turned).astype(BF16)
        fetch(jnp.minimum(c + 1, pieces - 1))
        result = ff_sum(mixed, gate_up[1], down[1]).astype(BF16)
        second[pl.ds(at, span), :] = result
        for t in range(tall.shape[0]):
            tall[t] = result[:, t * LANES:(t + 1) * LANES].astype(F32)
        side = [
            tall[t, pl.ds(j, piece, stride=FAN), :].astype(BF16)
            for j in range(FAN)
            for t in range(tall.shape[0])
        ]
        total = dot(jnp.concatenate(side, axis=1), pool[...])
        pooled[me, pl.ds(pl.multiple_of(c * piece, piece), piece), :] = total.astype(BF16)
        gather.own(c)
        gather.during(c)
        return carry

    lax.fori_loop(0, pieces, step, 0)
    small, width = own.shape
    size = width // CHEADS
    factor = size ** -0.5 * LOG2E
    part = 2 * LANES
    heads = part // size
    pairs = LANES // size
    head_of = lax.broadcasted_iota(jnp.int32, (small, part), 1) // size
    lane_head = lax.broadcasted_iota(jnp.int32, (small, LANES), 1) // size
    zero, one = jnp.zeros((), BF16), jnp.ones((), BF16)
    own[...] = pooled[me]
    queries[...] = dot(normed(pooled[me]), w_in[:, :width]).astype(BF16)
    top[...] = jnp.full(top.shape, -1e38, F32)
    value_sum[...] = jnp.zeros(value_sum.shape, F32)
    weight_sum[...] = jnp.zeros(weight_sum.shape, F32)

    def attend(i, carry):
        gather.before(i)
        packed = dot(normed(pooled[gather.block_of(i)]), w_in[:, width:]).astype(BF16)
        for g in range(width // part):
            at = g * part
            q = queries[:, at:at + part]
            k = packed[:, at:at + part]
            v = packed[:, width + at:width + at + part]
            results, scales = [], []
            for h in range(heads):
                mine = head_of == h
                s = dot_t(jnp.where(mine, q, zero), k)
                old = top[g * heads + h]
                m = jnp.maximum(old, jnp.max(s, axis=-1, keepdims=True))
                top[g * heads + h] = m
                tiled = jnp.concatenate([m] * (s.shape[1] // LANES), axis=1)
                e = jnp.exp2((s - tiled) * factor).astype(BF16)
                scales.append(jnp.exp2((old - m) * factor))
                results.append(dot(e, jnp.where(mine, v, one)))
            for t in range(part // LANES):
                lane = slice(t * LANES, (t + 1) * LANES)
                free = slice((1 - t) * LANES, (2 - t) * LANES)
                scale, value, total = None, None, None
                for h in range(t * pairs, (t + 1) * pairs):
                    here = (scales[h], results[h][:, lane], results[h][:, free])
                    if scale is None:
                        scale, value, total = here
                    else:
                        pick = lane_head >= h - t * pairs
                        scale = jnp.where(pick, here[0], scale)
                        value = jnp.where(pick, here[1], value)
                        total = jnp.where(pick, here[2], total)
                spot = slice(at + t * LANES, at + (t + 1) * LANES)
                value_sum[:, spot] = value_sum[:, spot] * scale + value
                weight_sum[:, spot] = weight_sum[:, spot] * scale + total
        return carry

    lax.fori_loop(0, GROUP, attend, 0)
    mixture[...] = (value_sum[...] / weight_sum[...]).astype(BF16)
    gather.finish()


def coarse_kernel(pooled, mixture, second, w_out, gate_up, down, unpool, out, lifted):
    rows = pooled.shape[0]
    mixed = (pooled[...].astype(F32) + dot(mixture[...], w_out[...])).astype(BF16)
    coarse = ff_sum(mixed, gate_up[...], down[...]).astype(BF16)
    up = normed(coarse)
    fine = out.shape[1]
    for j in range(FAN):
        part_up = dot(up, unpool[:, j * fine:(j + 1) * fine])
        for t in range(lifted.shape[0]):
            lifted[t, pl.ds(j, rows, stride=FAN), :] = part_up[:, t * LANES:(t + 1) * LANES]
    for c in range(out.shape[0] // BALL):
        at = c * BALL
        for t in range(lifted.shape[0]):
            lane = slice(t * LANES, (t + 1) * LANES)
            out[at:at + BALL, lane] = (
                second[at:at + BALL, lane].astype(F32) + lifted[t, at:at + BALL, :]
            ).astype(BF16)


VMEM = pl.BlockSpec(memory_space=pltpu.VMEM)
SMEM = pl.BlockSpec(memory_space=pltpu.SMEM)
DMA = pltpu.SemaphoreType.DMA


def local(
    points,
    rotated_slot,
    fine_attend_in,
    fine_attend_out,
    fine_gate_up,
    fine_down,
    pool_weight,
    coarse_attend_in,
    coarse_attend_out,
    coarse_gate_up,
    coarse_down,
    unpool_weight,
):
    rows, width = points.shape
    row_size = lax.axis_size("row")
    col_size = lax.axis_size("col")
    count = rows // BALL
    small = rows // FAN
    coarse_width = pool_weight.shape[1]
    lanes = LANES
    lines = rows // lanes
    mib = 1024 * 1024
    parts = width // LANES
    everyone = jax.ShapeDtypeStruct((row_size * rows * parts, LANES), F32)
    held = pltpu.VMEM((row_size, rows, width), BF16)
    scalars = jax.ShapeDtypeStruct((lines, lanes), jnp.int32)
    both = jax.ShapeDtypeStruct((2 * lines, lanes), jnp.int32)

    first, wide, inverse, route = pl.pallas_call(
        functools.partial(layer_one_kernel, col_size),
        out_shape=(jax.ShapeDtypeStruct((rows, width), BF16), everyone, both, scalars),
        in_specs=[pl.BlockSpec(memory_space=pltpu.HBM)] * 6,
        out_specs=(VMEM,) * 4,
        scratch_shapes=[
            held,
            pltpu.VMEM((row_size, lines, lanes), jnp.int32),
            pltpu.VMEM((rows + RAW * BALL, width), BF16),
            pltpu.VMEM(fine_attend_in.shape[1:], BF16),
            pltpu.VMEM(fine_attend_out.shape[1:], BF16),
            pltpu.VMEM(fine_gate_up.shape[1:], BF16),
            pltpu.VMEM(fine_down.shape[1:], BF16),
            DMA((6,)),
            DMA((3, count)),
            DMA((3, count)),
            DMA((3,)),
            DMA((3,)),
        ],
        compiler_params=pltpu.CompilerParams(
            collective_id=0, has_side_effects=True, vmem_limit_bytes=36 * mib
        ),
        name="layer_one",
    )(
        *(
            pltpu.with_memory_space_constraint(array, pltpu.HBM)
            for array in (
                points,
                rotated_slot.reshape(lines, lanes),
                fine_attend_in,
                fine_attend_out,
                fine_gate_up,
                fine_down,
            )
        )
    )

    turned = pl.pallas_call(
        turn_kernel,
        out_shape=everyone,
        in_specs=[VMEM, SMEM, VMEM, VMEM],
        out_specs=VMEM,
        scratch_shapes=[
            held,
            pltpu.VMEM((PAIR, BALL * parts, LANES), F32),
            DMA((3, count)),
            DMA((3, count)),
        ],
        compiler_params=pltpu.CompilerParams(
            collective_id=1, has_side_effects=True, vmem_limit_bytes=24 * mib
        ),
        name="turn",
    )(wide, inverse.reshape(-1), fine_attend_in, fine_attend_out)

    pieces = count // PAIR
    kinds = 10
    one = jax.ShapeDtypeStruct((small, coarse_width), BF16)
    totals = pltpu.VMEM((small, coarse_width), F32)
    second, *coarse_parts = pl.pallas_call(
        layer_two_kernel,
        out_shape=(jax.ShapeDtypeStruct((rows, width), BF16), one, one),
        in_specs=[VMEM, VMEM, SMEM, VMEM, VMEM, VMEM, VMEM],
        out_specs=(VMEM,) * 3,
        scratch_shapes=[
            pltpu.VMEM((GROUP, small, coarse_width), BF16),
            pltpu.VMEM((PAIR, BALL * parts, LANES), F32),
            pltpu.VMEM((parts, PAIR * BALL, LANES), F32),
            pltpu.VMEM((small, coarse_width), BF16),
            pltpu.VMEM((CHEADS, small, LANES), F32),
            totals,
            totals,
            DMA((kinds, pieces)),
            DMA((GROUP, pieces)),
        ],
        compiler_params=pltpu.CompilerParams(
            collective_id=2, has_side_effects=True, vmem_limit_bytes=24 * mib
        ),
        name="layer_two",
    )(first, turned, route.reshape(-1), fine_gate_up, fine_down, pool_weight, coarse_attend_in)

    return pl.pallas_call(
        coarse_kernel,
        out_shape=jax.ShapeDtypeStruct((rows, width), BF16),
        in_specs=[VMEM] * 7,
        out_specs=VMEM,
        scratch_shapes=[
            pltpu.VMEM((width // LANES, rows, LANES), F32),
        ],
        compiler_params=pltpu.CompilerParams(vmem_limit_bytes=22 * mib),
        name="coarse",
    )(
        *coarse_parts,
        second,
        coarse_attend_out,
        coarse_gate_up,
        coarse_down,
        unpool_weight,
    )


def solution(mesh):
    split = P(("row", "col"), None)
    placed = (split, P(("row", "col"))) + (P(),) * 10
    return jax.shard_map(local, mesh=mesh, in_specs=placed, out_specs=split, check_vma=False)
```

```python
import functools
import math

import jax
import jax.numpy as jnp
from jax import lax
from jax.experimental import pallas as pl
from jax.experimental.pallas import tpu as pltpu
from jax.sharding import PartitionSpec as P

HEADS = 8
CHEADS = 8
BALL = 256
GROUP = 8
FAN = 8
LANES = 128
EPS = 1e-06
F32 = jnp.float32
BF16 = jnp.bfloat16
LOG2E = 1.4426950408889634


def dot(a, b):
    return jnp.dot(a, b, preferred_element_type=F32)


def dot_t(a, b):
    return lax.dot_general(a, b, (((1,), (1,)), ((), ())), preferred_element_type=F32)


def normed(x):
    wide = x.astype(F32)
    return (wide * lax.rsqrt(jnp.mean(wide * wide, axis=-1, keepdims=True) + EPS)).astype(BF16)


def ff_sum(x, gate_up, down):
    both = dot(normed(x), gate_up)
    half = both.shape[1] // 2
    g = both[:, :half]
    hidden = ((0.5 * g) * (1.0 + jnp.tanh(0.5 * g)) * both[:, half:]).astype(BF16)
    return x.astype(F32) + dot(hidden, down)


def ball_mixture(packed):
    rows, width = packed.shape[0], packed.shape[1] // 3
    q, k, v = packed[:, :width], packed[:, width:2 * width], packed[:, 2 * width:]
    size = width // HEADS
    factor = size ** -0.5 * LOG2E
    half = width // 2
    head_of = lax.broadcasted_iota(jnp.int32, (rows, width), 1) // size
    zero = jnp.zeros((), BF16)
    parts = []
    for g in range(2):
        both = None
        for h in range(g * HEADS // 2, (g + 1) * HEADS // 2):
            mine = head_of == h
            s = dot_t(jnp.where(mine, q, zero), k)
            m = jnp.max(s, axis=-1, keepdims=True)
            e = jnp.exp2((s - m) * factor).astype(BF16)
            mine = mine[:, g * half:(g + 1) * half]
            value = jnp.concatenate(
                (
                    jnp.where(mine, v[:, g * half:(g + 1) * half], zero),
                    jnp.where(mine, jnp.ones((), BF16), zero),
                ),
                axis=1,
            )
            r = dot(e, value)
            both = r if both is None else both + r
        parts.append((both[:, :half] / both[:, half:]).astype(BF16))
    return jnp.concatenate(parts, axis=1)


def fine_attention(n, w_in, w_out):
    packed = dot(n, w_in).astype(BF16)
    balls = [ball_mixture(packed[i:i + BALL]) for i in range(0, n.shape[0], BALL)]
    return dot(jnp.concatenate(balls, axis=0), w_out)


def row_peers():
    me = lax.axis_index("row")
    near = me + 1 - 2 * (me % 2)
    far = me + 2 - 4 * ((me // 2) % 2)
    return me, near, far


def greet(peers, axis):
    barrier = pltpu.get_barrier_semaphore()
    for peer in peers:
        pl.semaphore_signal(
            barrier, inc=1, device_id={axis: peer}, device_id_type=pl.DeviceIdType.MESH
        )


def meet(count):
    pl.semaphore_wait(pltpu.get_barrier_semaphore(), count)


PAIR = 2
RAW = 2
SENT = 4
SINGLE = 2


class RowGather:
    def __init__(self, held, wide, send, recv):
        self.held, self.wide = held, wide
        self.send, self.recv = send, recv
        self.me, self.near, self.far = row_peers()
        self.last = self.far + self.near - self.me

    def copy(self, kind, c, block, peer):
        spot = self.held.at[block, pl.ds(c * BALL, BALL)]
        return self.between(kind, c, spot, spot, peer)

    def between(self, kind, c, source, target, peer):
        return pltpu.make_async_remote_copy(
            src_ref=source,
            dst_ref=target,
            send_sem=self.send.at[kind, c],
            recv_sem=self.recv.at[kind, c],
            device_id={"row": peer},
            device_id_type=pl.DeviceIdType.MESH,
        )

    def put(self, block, c, value):
        rows = self.held.shape[1]
        self.held[block, pl.ds(pl.multiple_of(c * BALL, BALL), BALL), :] = value
        self.widen(block, c, value)

    def widen(self, block, c, value):
        rows, width = self.held.shape[1:]
        parts = width // LANES
        at = pl.multiple_of((block * rows + c * BALL) * parts, BALL * parts)
        for t in range(parts):
            self.wide[pl.ds(at + t, BALL, stride=parts), :] = value[
                :, t * LANES:(t + 1) * LANES
            ].astype(F32)

    def arrived(self, block, c):
        at = pl.multiple_of(c * BALL, BALL)
        self.widen(block, c, self.held[block, pl.ds(at, BALL), :])

    def to_far(self, c):
        self.copy(0, c, self.me, self.far).start()

    def to_near(self, c):
        self.copy(1, c, self.me, self.near).start()

    def far_to_near(self, c):
        self.copy(2, c, self.far, self.near).start()

    def relay(self, c):
        self.copy(0, c, self.far, self.far).wait_recv()
        self.far_to_near(c)
        self.arrived(self.far, c)

    def from_near(self, c):
        self.copy(1, c, self.near, self.near).wait_recv()
        self.arrived(self.near, c)

    def from_last(self, c):
        self.copy(2, c, self.last, self.near).wait_recv()
        self.arrived(self.last, c)


def each(start, stop, do):
    def body(c, carry):
        do(c)
        return carry

    lax.fori_loop(start, stop, body, 0)


def positions(slot_all, targets, col_size):
    lines, lanes = slot_all.shape[1:]
    rows = lines * lanes
    row_id = lax.broadcasted_iota(jnp.int32, (lines, lanes), 0)
    lane_id = lax.broadcasted_iota(jnp.int32, (lines, lanes), 1).astype(F32)
    sub_id = lax.broadcasted_iota(jnp.int32, (lanes, lanes), 0)
    left, right = [], []
    for r in range(slot_all.shape[0]):
        for c in range(lines):
            line = slot_all[r, c:c + 1, :]
            owner, spot = line // (rows * col_size), line % rows
            parts = []
            for target in targets:
                hit = row_id == jnp.where(owner == target, spot // lanes, lines)
                parts += [jnp.where(hit, float(r * lines + c), 0.0), jnp.where(hit, lane_id, 0.0)]
            left.append(jnp.concatenate(parts, axis=0).astype(BF16))
            right.append(jnp.where(sub_id == spot % lanes, 1.0, 0.0).astype(BF16))
    found = dot_t(jnp.concatenate(left, axis=1), jnp.concatenate(right, axis=1))
    return [
        (found[at:at + lines] * lanes + found[at + lines:at + 2 * lines]).astype(jnp.int32)
        for at in range(0, found.shape[0], 2 * lines)
    ]


def layer_one_kernel(
    col_size, points_hbm, slots_hbm, w_in_hbm, w_out_hbm, gate_up_hbm, down_hbm, out, wide,
    inverse, route, held, slot_all, points, w_in, w_out, gate_up, down, loaded, send, recv,
    s_send, s_recv,
):
    rows = out.shape[0]
    count = rows // BALL
    keep = count - RAW
    me, near, far = row_peers()
    other = far + near - me
    loads = [
        pltpu.make_async_copy(source, target, loaded.at[i])
        for i, (source, target) in enumerate(
            (
                (slots_hbm, slot_all.at[me]),
                (points_hbm, points.at[pl.ds(0, rows)]),
                (w_in_hbm.at[0], w_in),
                (w_out_hbm.at[0], w_out),
                (gate_up_hbm.at[0], gate_up),
                (down_hbm.at[0], down),
            )
        )
    ]
    greet((near, far, other), "row")
    for load in loads:
        load.start()
    meet(3)
    gather = RowGather(held, wide, send, recv)

    def raw_copy(c):
        return gather.between(
            0,
            c,
            points_hbm.at[pl.ds(c * BALL, BALL)],
            points.at[pl.ds((c + RAW) * BALL, BALL)],
            far,
        )

    for c in range(keep, count):
        raw_copy(c).start()
    loads[0].wait()

    def slot_copy(kind, block, peer):
        return pltpu.make_async_remote_copy(
            src_ref=slot_all.at[me],
            dst_ref=slot_all.at[block],
            send_sem=s_send.at[kind],
            recv_sem=s_recv.at[kind],
            device_id={"row": peer},
            device_id_type=pl.DeviceIdType.MESH,
        )

    for kind, peer in enumerate((near, far, other)):
        slot_copy(kind, me, peer).start()
    slots = slot_all[me]
    parts = out.shape[1] // LANES
    route[...] = (slots // (rows * col_size) * rows + slots % rows) * parts
    for load in loads[1:]:
        load.wait()

    lines = slot_all.shape[1]
    own_steps = count // PAIR
    sent_steps = keep // PAIR
    span = PAIR * BALL

    def step(s, carry):
        @pl.when(s == own_steps)
        def _():
            for c in range(keep, count):
                raw_copy(c).wait_recv()

        u = points[pl.ds(pl.multiple_of(s * span, span), span), :]
        mixed = (u.astype(F32) + fine_attention(normed(u), w_in[...], w_out[...])).astype(BF16)
        value = ff_sum(mixed, gate_up[...], down[...]).astype(BF16)

        @pl.when(s < own_steps)
        def _():
            out[pl.ds(pl.multiple_of(s * span, span), span), :] = value

        unit = normed(value)
        again = s // own_steps
        block = me + (far - me) * again
        first = s * PAIR - RAW * again
        for i in range(PAIR):
            gather.put(block, first + i, unit[i * BALL:(i + 1) * BALL])

            @pl.when(s < sent_steps)
            def _():
                gather.to_far(first + i)

            @pl.when(s < own_steps)
            def _():
                gather.to_near(first + i)

            @pl.when(s == own_steps)
            def _():
                gather.far_to_near(first + i)

        @pl.when(s >= 1)
        def _():
            for i in range(PAIR):
                gather.from_near((s - 1) * PAIR + i)

        @pl.when(s == 1)
        def _():
            for kind, peer in enumerate((near, far, other)):
                slot_copy(kind, peer, peer).wait()
            mine, theirs = positions(slot_all, (me, far), col_size)
            inverse[:lines] = mine * parts
            inverse[lines:] = theirs * parts

        @pl.when(s >= own_steps - 1)
        def _():
            for i in range(PAIR):
                gather.relay((s - own_steps + 1) * PAIR + i)

        return carry

    lax.fori_loop(0, own_steps + 1, step, 0)
    done = 2 * PAIR
    each(keep, count, gather.from_last)
    each(0, done - 1, gather.from_last)

    def tail(c):
        gather.relay(c)
        gather.from_last(c - 1)

    each(done, keep, tail)
    gather.from_last(keep - 1)

    def end(c):
        gather.copy(1, c, me, near).wait_send()
        gather.copy(2, c, far, near).wait_send()

    each(0, count, end)
    each(0, keep, lambda c: gather.copy(0, c, me, far).wait_send())
    for c in range(keep, count):
        raw_copy(c).wait_send()


def take_rows(wide, index, base, taken):
    parts = taken.shape[0] // BALL
    for i in range(BALL):
        taken[pl.ds(i * parts, parts), :] = wide[pl.ds(index[base + i], parts), :]


def taken_rows(taken):
    parts = taken.shape[0] // BALL
    return jnp.concatenate(
        [taken[pl.ds(t, BALL, stride=parts), :] for t in range(parts)], axis=1
    )


def turn_kernel(source, index, w_in, w_out, wide, held, taken, send, recv):
    rows = held.shape[1]
    count = rows // BALL
    total = 2 * count - SENT
    me, near, far = row_peers()
    greet((near, far), "row")
    gather = RowGather(held, wide, send, recv)

    def fetch(n):
        for i in range(PAIR):
            ball = n + i
            take_rows(source, index, (ball + SENT * (ball // count)) * BALL, taken.at[i])

    def work(n, size):
        u = jnp.concatenate([taken_rows(taken.at[i]) for i in range(size)], axis=0).astype(BF16)
        fetch(jnp.minimum(n + size, total - PAIR))
        value = fine_attention(u, w_in[1], w_out[1]).astype(BF16)

        @pl.when(n == 0)
        def _():
            meet(2)

        again = n // count
        block = me + (far - me) * again
        first = n + (SENT - count) * again
        for i in range(size):
            gather.put(block, first + i, value[i * BALL:(i + 1) * BALL])

            @pl.when(n < SENT)
            def _():
                gather.to_far(first + i)

            @pl.when(n < count)
            def _():
                gather.to_near(first + i)

            @pl.when(n >= count)
            def _():
                gather.far_to_near(first + i)

    fetch(0)
    each(0, SINGLE, lambda n: work(n, 1))

    def step(n):
        work(n, PAIR)

        @pl.when(n <= count)
        def _():
            for i in range(PAIR):
                gather.from_near(n - PAIR + i)

        @pl.when(n > count)
        def _():
            for i in range(PAIR):
                gather.from_last(n - PAIR + SENT - count + i)

        for c in range(PAIR):
            @pl.when(n == SINGLE + (c + 1) * PAIR)
            def _():
                gather.relay(c)

    each(0, (total - SINGLE) // PAIR, lambda p: step(SINGLE + p * PAIR))
    each(PAIR, SENT, gather.relay)
    each(count - PAIR, count, gather.from_last)
    each(0, SENT, gather.from_last)

    def end(c):
        gather.copy(1, c, me, near).wait_send()
        gather.copy(2, c, far, near).wait_send()

    each(0, count, end)
    each(0, SENT, lambda c: gather.copy(0, c, me, far).wait_send())


class ColGather:
    def __init__(self, pooled, send, recv):
        self.pooled, self.send, self.recv = pooled, send, recv
        self.pieces = recv.shape[1]
        self.half = self.pieces // 2
        self.piece = pooled.shape[1] // self.pieces
        col = lax.axis_index("col")
        me = col % GROUP
        self.me, self.base = me, col - me
        side, line = me % 2, me // 2
        self.over = 1 - 2 * side
        self.flip = me + self.over
        self.pair = me + 2 - 4 * (line % 2)
        self.across = (GROUP // 2 - 1 - line) * 2 + side
        self.second = side + 4 - 2 * (line // 2)
        self.third = side + 6 - 6 * (line // 2)
        self.inner = (line == 1) | (line == 2)
        self.outer = (line == 0) | (line == 3)

    def copy(self, kind, c, block, peer):
        spot = self.pooled.at[block, pl.ds(c * self.piece, self.piece)]
        return pltpu.make_async_remote_copy(
            src_ref=spot,
            dst_ref=spot,
            send_sem=self.send.at[kind, c],
            recv_sem=self.recv.at[block, c],
            device_id={"col": self.base + peer},
            device_id_type=pl.DeviceIdType.MESH,
        )

    def moves(self, kind):
        return (
            (self.me, self.pair),
            (self.me, self.flip),
            (self.me, self.across),
            (self.pair, self.across),
            (self.second, self.pair),
            (self.third, self.pair),
            (self.pair, self.flip),
            (self.second, self.flip),
            (self.third, self.flip),
            (self.flip, self.pair),
        )[kind]

    def go(self, kind, c):
        self.copy(kind, c, *self.moves(kind)).start()

    def landed(self, block, c):
        self.copy(0, c, block, self.pair).wait_recv()

    def all_landed(self, block):
        each(0, self.pieces, lambda c: self.landed(block, c))

    def own(self, c):
        self.go(0, c)
        self.go(1, c)

        @pl.when(self.inner)
        def _():
            self.go(2, c)

    def pass_pair(self, c):
        self.landed(self.pair, c)

        @pl.when(self.inner)
        def _():
            self.go(3, c)

        @pl.when(c < self.half)
        def _():
            self.go(6, c)

    def pass_second(self, c):
        self.landed(self.second, c)

        @pl.when(self.inner)
        def _():
            self.go(4, c)

        self.go(7, c)

    def pass_third(self, c):
        self.landed(self.third, c)

        @pl.when(self.inner)
        def _():
            self.go(5, c)

        self.go(8, c)

    def pass_flip(self):
        each(self.half, self.pieces, lambda c: self.go(9, c))

    def block_of(self, i):
        order = (
            self.me,
            self.flip,
            self.pair,
            self.second,
            self.second + self.over,
            self.third,
            self.pair + self.over,
            self.third + self.over,
        )
        block = order[0]
        for at in range(1, GROUP):
            block = block + (order[at] - order[at - 1]) * ((i + GROUP - at) // GROUP)
        return block

    def unit(self, i):
        half = self.half * self.piece
        late, last = (i + 2) // GROUP, (i + 1) // GROUP
        low = self.block_of(i - last)
        high = self.block_of(i + late - last)
        spots = (low, half * last), (high, half * (1 - late + last))
        return jnp.concatenate(
            [self.pooled[block, pl.ds(pl.multiple_of(at, half), half), :] for block, at in spots],
            axis=0,
        )

    def before(self, i):
        last = self.pieces - 1

        @pl.when(i == 1)
        def _():
            self.pass_pair(last)

        @pl.when((i == 1) & self.inner)
        def _():
            self.pass_second(last)
            self.pass_third(1)

        @pl.when((i == 1) & self.outer)
        def _():
            self.pass_second(1)

        @pl.when(i == 1)
        def _():
            self.all_landed(self.flip)

        @pl.when((i == 1) & self.outer)
        def _():
            self.pass_flip()

        @pl.when((i == 2) & self.inner)
        def _():
            self.pass_third(2)

        @pl.when((i == 3) & self.inner)
        def _():
            each(3, self.pieces, self.pass_third)
            self.pass_flip()

        @pl.when((i == 3) & self.outer)
        def _():
            each(2, self.pieces, self.pass_second)

        @pl.when((i == 4) & self.outer)
        def _():
            each(0, 2, self.pass_third)

        @pl.when(i == 4)
        def _():
            self.all_landed(self.second + self.over)

        @pl.when((i == 5) & self.outer)
        def _():
            each(2, self.pieces, self.pass_third)

        for late in range(2):
            @pl.when(i == GROUP - 2 + late)
            def _():
                for block in (self.pair + self.over, self.third + self.over):
                    each(
                        late * self.half,
                        (1 + late) * self.half,
                        lambda c: self.landed(block, c),
                    )

    def during(self, c):
        @pl.when(c >= 1)
        def _():
            self.pass_pair(c - 1)

        @pl.when((c >= 1) & self.inner)
        def _():
            self.pass_second(c - 1)

        @pl.when((c == self.pieces - 1) & self.inner)
        def _():
            self.pass_third(0)

        @pl.when((c == self.pieces - 1) & self.outer)
        def _():
            self.pass_second(0)

    def finish(self):
        def sent(kind):
            return lambda c: self.copy(kind, c, *self.moves(kind)).wait_send()

        for kind in (0, 1, 7, 8):
            each(0, self.pieces, sent(kind))
        each(0, self.half, sent(6))
        each(self.half, self.pieces, sent(9))

        @pl.when(self.inner)
        def _():
            for kind in (2, 3, 4, 5):
                each(0, self.pieces, sent(kind))


def layer_two_kernel(
    first, wide, index, gate_up, down, pool, w_in, second, own, mixture, pooled, taken, tall,
    queries, top, value_sum, weight_sum, send, recv
):
    rows = second.shape[0]
    span = PAIR * BALL
    gather = ColGather(pooled, send, recv)
    me, pieces, piece = gather.me, gather.pieces, gather.piece
    greet([gather.base + p for p in (gather.flip, gather.pair, gather.across)], "col")

    def fetch(c):
        for i in range(PAIR):
            take_rows(wide, index, (c * PAIR + i) * BALL, taken.at[i])

    fetch(0)

    def step(c, carry):
        at = pl.multiple_of(c * span, span)
        turned = jnp.concatenate([taken_rows(taken.at[i]) for i in range(PAIR)], axis=0)
        mixed = (first[pl.ds(at, span), :].astype(F32) + turned).astype(BF16)
        fetch(jnp.minimum(c + 1, pieces - 1))
        result = ff_sum(mixed, gate_up[1], down[1]).astype(BF16)
        second[pl.ds(at, span), :] = result
        for t in range(tall.shape[0]):
            tall[t] = result[:, t * LANES:(t + 1) * LANES].astype(F32)
        side = [
            tall[t, pl.ds(j, piece, stride=FAN), :].astype(BF16)
            for j in range(FAN)
            for t in range(tall.shape[0])
        ]
        total = dot(jnp.concatenate(side, axis=1), pool[...])
        pooled[me, pl.ds(pl.multiple_of(c * piece, piece), piece), :] = total.astype(BF16)

        @pl.when(c == 0)
        def _():
            meet(3)

        gather.own(c)
        gather.during(c)
        return carry

    lax.fori_loop(0, pieces, step, 0)
    small, width = own.shape
    size = width // CHEADS
    factor = size ** -0.5 * LOG2E
    part = 2 * LANES
    heads = part // size
    pairs = LANES // size
    head_of = lax.broadcasted_iota(jnp.int32, (small, part), 1) // size
    lane_head = lax.broadcasted_iota(jnp.int32, (small, LANES), 1) // size
    zero, one = jnp.zeros((), BF16), jnp.ones((), BF16)
    own[...] = pooled[me]
    queries[...] = dot(normed(pooled[me]), w_in[:, :width]).astype(BF16)
    top[...] = jnp.full(top.shape, -1e38, F32)
    value_sum[...] = jnp.zeros(value_sum.shape, F32)
    weight_sum[...] = jnp.zeros(weight_sum.shape, F32)

    def attend(i, carry):
        gather.before(i)
        packed = dot(normed(gather.unit(i)), w_in[:, width:]).astype(BF16)
        for g in range(width // part):
            at = g * part
            q = queries[:, at:at + part]
            k = packed[:, at:at + part]
            v = packed[:, width + at:width + at + part]
            results, scales = [], []
            for h in range(heads):
                mine = head_of == h
                s = dot_t(jnp.where(mine, q, zero), k)
                old = top[g * heads + h]
                m = jnp.maximum(old, jnp.max(s, axis=-1, keepdims=True))
                top[g * heads + h] = m
                tiled = jnp.concatenate([m] * (s.shape[1] // LANES), axis=1)
                e = jnp.exp2((s - tiled) * factor).astype(BF16)
                scales.append(jnp.exp2((old - m) * factor))
                results.append(dot(e, jnp.where(mine, v, one)))
            for t in range(part // LANES):
                lane = slice(t * LANES, (t + 1) * LANES)
                free = slice((1 - t) * LANES, (2 - t) * LANES)
                scale, value, total = None, None, None
                for h in range(t * pairs, (t + 1) * pairs):
                    here = (scales[h], results[h][:, lane], results[h][:, free])
                    if scale is None:
                        scale, value, total = here
                    else:
                        pick = lane_head >= h - t * pairs
                        scale = jnp.where(pick, here[0], scale)
                        value = jnp.where(pick, here[1], value)
                        total = jnp.where(pick, here[2], total)
                spot = slice(at + t * LANES, at + (t + 1) * LANES)
                value_sum[:, spot] = value_sum[:, spot] * scale + value
                weight_sum[:, spot] = weight_sum[:, spot] * scale + total
        return carry

    lax.fori_loop(0, GROUP, attend, 0)
    mixture[...] = (value_sum[...] / weight_sum[...]).astype(BF16)
    gather.finish()


def coarse_kernel(pooled, mixture, second, w_out, gate_up, down, unpool, out, lifted):
    rows = pooled.shape[0]
    mixed = (pooled[...].astype(F32) + dot(mixture[...], w_out[...])).astype(BF16)
    coarse = ff_sum(mixed, gate_up[...], down[...]).astype(BF16)
    up = normed(coarse)
    fine = out.shape[1]
    for j in range(FAN):
        part_up = dot(up, unpool[:, j * fine:(j + 1) * fine])
        for t in range(lifted.shape[0]):
            lifted[t, pl.ds(j, rows, stride=FAN), :] = part_up[:, t * LANES:(t + 1) * LANES]
    for c in range(out.shape[0] // BALL):
        at = c * BALL
        for t in range(lifted.shape[0]):
            lane = slice(t * LANES, (t + 1) * LANES)
            out[at:at + BALL, lane] = (
                second[at:at + BALL, lane].astype(F32) + lifted[t, at:at + BALL, :]
            ).astype(BF16)


VMEM = pl.BlockSpec(memory_space=pltpu.VMEM)
SMEM = pl.BlockSpec(memory_space=pltpu.SMEM)
DMA = pltpu.SemaphoreType.DMA


def local(
    points,
    rotated_slot,
    fine_attend_in,
    fine_attend_out,
    fine_gate_up,
    fine_down,
    pool_weight,
    coarse_attend_in,
    coarse_attend_out,
    coarse_gate_up,
    coarse_down,
    unpool_weight,
):
    rows, width = points.shape
    row_size = lax.axis_size("row")
    col_size = lax.axis_size("col")
    count = rows // BALL
    small = rows // FAN
    coarse_width = pool_weight.shape[1]
    lanes = LANES
    lines = rows // lanes
    mib = 1024 * 1024
    parts = width // LANES
    everyone = jax.ShapeDtypeStruct((row_size * rows * parts, LANES), F32)
    held = pltpu.VMEM((row_size, rows, width), BF16)
    scalars = jax.ShapeDtypeStruct((lines, lanes), jnp.int32)
    both = jax.ShapeDtypeStruct((2 * lines, lanes), jnp.int32)

    first, wide, inverse, route = pl.pallas_call(
        functools.partial(layer_one_kernel, col_size),
        out_shape=(jax.ShapeDtypeStruct((rows, width), BF16), everyone, both, scalars),
        in_specs=[pl.BlockSpec(memory_space=pltpu.HBM)] * 6,
        out_specs=(VMEM,) * 4,
        scratch_shapes=[
            held,
            pltpu.VMEM((row_size, lines, lanes), jnp.int32),
            pltpu.VMEM((rows + RAW * BALL, width), BF16),
            pltpu.VMEM(fine_attend_in.shape[1:], BF16),
            pltpu.VMEM(fine_attend_out.shape[1:], BF16),
            pltpu.VMEM(fine_gate_up.shape[1:], BF16),
            pltpu.VMEM(fine_down.shape[1:], BF16),
            DMA((6,)),
            DMA((3, count)),
            DMA((3, count)),
            DMA((3,)),
            DMA((3,)),
        ],
        compiler_params=pltpu.CompilerParams(
            collective_id=0, has_side_effects=True, vmem_limit_bytes=36 * mib
        ),
        name="layer_one",
    )(
        *(
            pltpu.with_memory_space_constraint(array, pltpu.HBM)
            for array in (
                points,
                rotated_slot.reshape(lines, lanes),
                fine_attend_in,
                fine_attend_out,
                fine_gate_up,
                fine_down,
            )
        )
    )

    turned = pl.pallas_call(
        turn_kernel,
        out_shape=everyone,
        in_specs=[VMEM, SMEM, VMEM, VMEM],
        out_specs=VMEM,
        scratch_shapes=[
            held,
            pltpu.VMEM((PAIR, BALL * parts, LANES), F32),
            DMA((3, count)),
            DMA((3, count)),
        ],
        compiler_params=pltpu.CompilerParams(
            collective_id=1, has_side_effects=True, vmem_limit_bytes=24 * mib
        ),
        name="turn",
    )(wide, inverse.reshape(-1), fine_attend_in, fine_attend_out)

    pieces = count // PAIR
    kinds = 10
    one = jax.ShapeDtypeStruct((small, coarse_width), BF16)
    totals = pltpu.VMEM((small, coarse_width), F32)
    second, *coarse_parts = pl.pallas_call(
        layer_two_kernel,
        out_shape=(jax.ShapeDtypeStruct((rows, width), BF16), one, one),
        in_specs=[VMEM, VMEM, SMEM, VMEM, VMEM, VMEM, VMEM],
        out_specs=(VMEM,) * 3,
        scratch_shapes=[
            pltpu.VMEM((GROUP, small, coarse_width), BF16),
            pltpu.VMEM((PAIR, BALL * parts, LANES), F32),
            pltpu.VMEM((parts, PAIR * BALL, LANES), F32),
            pltpu.VMEM((small, coarse_width), BF16),
            pltpu.VMEM((CHEADS, small, LANES), F32),
            totals,
            totals,
            DMA((kinds, pieces)),
            DMA((GROUP, pieces)),
        ],
        compiler_params=pltpu.CompilerParams(
            collective_id=2, has_side_effects=True, vmem_limit_bytes=24 * mib
        ),
        name="layer_two",
    )(first, turned, route.reshape(-1), fine_gate_up, fine_down, pool_weight, coarse_attend_in)

    return pl.pallas_call(
        coarse_kernel,
        out_shape=jax.ShapeDtypeStruct((rows, width), BF16),
        in_specs=[VMEM] * 7,
        out_specs=VMEM,
        scratch_shapes=[
            pltpu.VMEM((width // LANES, rows, LANES), F32),
        ],
        compiler_params=pltpu.CompilerParams(vmem_limit_bytes=22 * mib),
        name="coarse",
    )(
        *coarse_parts,
        second,
        coarse_attend_out,
        coarse_gate_up,
        coarse_down,
        unpool_weight,
    )


def solution(mesh):
    split = P(("row", "col"), None)
    placed = (split, P(("row", "col"))) + (P(),) * 10
    return jax.shard_map(local, mesh=mesh, in_specs=placed, out_specs=split, check_vma=False)
```

```python
import functools
import math

import jax
import jax.numpy as jnp
from jax import lax
from jax.experimental import pallas as pl
from jax.experimental.pallas import tpu as pltpu
from jax.sharding import PartitionSpec as P

HEADS = 8
CHEADS = 8
BALL = 256
GROUP = 8
FAN = 8
LANES = 128
EPS = 1e-06
F32 = jnp.float32
BF16 = jnp.bfloat16
LOG2E = 1.4426950408889634


def dot(a, b):
    return jnp.dot(a, b, preferred_element_type=F32)


def dot_t(a, b):
    return lax.dot_general(a, b, (((1,), (1,)), ((), ())), preferred_element_type=F32)


def normed(x):
    wide = x.astype(F32)
    return (wide * lax.rsqrt(jnp.mean(wide * wide, axis=-1, keepdims=True) + EPS)).astype(BF16)


def ff_sum(x, gate_up, down):
    both = dot(normed(x), gate_up)
    half = both.shape[1] // 2
    g = both[:, :half]
    hidden = ((0.5 * g) * (1.0 + jnp.tanh(0.5 * g)) * both[:, half:]).astype(BF16)
    return x.astype(F32) + dot(hidden, down)


def ball_mixture(packed):
    rows, width = packed.shape[0], packed.shape[1] // 3
    q, k, v = packed[:, :width], packed[:, width:2 * width], packed[:, 2 * width:]
    size = width // HEADS
    factor = size ** -0.5 * LOG2E
    half = width // 2
    head_of = lax.broadcasted_iota(jnp.int32, (rows, width), 1) // size
    zero = jnp.zeros((), BF16)
    parts = []
    for g in range(2):
        both = None
        for h in range(g * HEADS // 2, (g + 1) * HEADS // 2):
            mine = head_of == h
            s = dot_t(jnp.where(mine, q, zero), k)
            m = jnp.max(s, axis=-1, keepdims=True)
            e = jnp.exp2((s - m) * factor).astype(BF16)
            mine = mine[:, g * half:(g + 1) * half]
            value = jnp.concatenate(
                (
                    jnp.where(mine, v[:, g * half:(g + 1) * half], zero),
                    jnp.where(mine, jnp.ones((), BF16), zero),
                ),
                axis=1,
            )
            r = dot(e, value)
            both = r if both is None else both + r
        parts.append((both[:, :half] / both[:, half:]).astype(BF16))
    return jnp.concatenate(parts, axis=1)


def fine_attention(n, w_in, w_out):
    packed = dot(n, w_in).astype(BF16)
    balls = [ball_mixture(packed[i:i + BALL]) for i in range(0, n.shape[0], BALL)]
    return dot(jnp.concatenate(balls, axis=0), w_out)


def row_peers():
    me = lax.axis_index("row")
    near = me + 1 - 2 * (me % 2)
    far = me + 2 - 4 * ((me // 2) % 2)
    return me, near, far


def greet(peers, axis):
    barrier = pltpu.get_barrier_semaphore()
    for peer in peers:
        pl.semaphore_signal(
            barrier, inc=1, device_id={axis: peer}, device_id_type=pl.DeviceIdType.MESH
        )


def meet(count):
    pl.semaphore_wait(pltpu.get_barrier_semaphore(), count)


PAIR = 2
RAW = 2
SENT = 3
ALONE = 1


class RowGather:
    def __init__(self, held, wide, send, recv):
        self.held, self.wide = held, wide
        self.send, self.recv = send, recv
        self.me, self.near, self.far = row_peers()
        self.last = self.far + self.near - self.me

    def copy(self, kind, c, block, peer):
        spot = self.held.at[block, pl.ds(c * BALL, BALL)]
        return self.between(kind, c, spot, spot, peer)

    def between(self, kind, c, source, target, peer):
        return pltpu.make_async_remote_copy(
            src_ref=source,
            dst_ref=target,
            send_sem=self.send.at[kind, c],
            recv_sem=self.recv.at[kind, c],
            device_id={"row": peer},
            device_id_type=pl.DeviceIdType.MESH,
        )

    def put(self, block, c, value):
        rows = self.held.shape[1]
        self.held[block, pl.ds(pl.multiple_of(c * BALL, BALL), BALL), :] = value
        self.widen(block, c, value)

    def widen(self, block, c, value):
        rows, width = self.held.shape[1:]
        parts = width // LANES
        at = pl.multiple_of((block * rows + c * BALL) * parts, BALL * parts)
        for t in range(parts):
            self.wide[pl.ds(at + t, BALL, stride=parts), :] = value[
                :, t * LANES:(t + 1) * LANES
            ].astype(F32)

    def arrived(self, block, c):
        at = pl.multiple_of(c * BALL, BALL)
        self.widen(block, c, self.held[block, pl.ds(at, BALL), :])

    def to_far(self, c):
        self.copy(0, c, self.me, self.far).start()

    def to_near(self, c):
        self.copy(1, c, self.me, self.near).start()

    def far_to_near(self, c):
        self.copy(2, c, self.far, self.near).start()

    def relay(self, c):
        self.copy(0, c, self.far, self.far).wait_recv()
        self.far_to_near(c)
        self.arrived(self.far, c)

    def from_near(self, c):
        self.copy(1, c, self.near, self.near).wait_recv()
        self.arrived(self.near, c)

    def from_last(self, c):
        self.copy(2, c, self.last, self.near).wait_recv()
        self.arrived(self.last, c)


def each(start, stop, do):
    def body(c, carry):
        do(c)
        return carry

    lax.fori_loop(start, stop, body, 0)


def positions(slot_all, targets, col_size):
    lines, lanes = slot_all.shape[1:]
    rows = lines * lanes
    row_id = lax.broadcasted_iota(jnp.int32, (lines, lanes), 0)
    lane_id = lax.broadcasted_iota(jnp.int32, (lines, lanes), 1).astype(F32)
    sub_id = lax.broadcasted_iota(jnp.int32, (lanes, lanes), 0)
    left, right = [], []
    for r in range(slot_all.shape[0]):
        for c in range(lines):
            line = slot_all[r, c:c + 1, :]
            owner, spot = line // (rows * col_size), line % rows
            parts = []
            for target in targets:
                hit = row_id == jnp.where(owner == target, spot // lanes, lines)
                parts += [jnp.where(hit, float(r * lines + c), 0.0), jnp.where(hit, lane_id, 0.0)]
            left.append(jnp.concatenate(parts, axis=0).astype(BF16))
            right.append(jnp.where(sub_id == spot % lanes, 1.0, 0.0).astype(BF16))
    found = dot_t(jnp.concatenate(left, axis=1), jnp.concatenate(right, axis=1))
    return [
        (found[at:at + lines] * lanes + found[at + lines:at + 2 * lines]).astype(jnp.int32)
        for at in range(0, found.shape[0], 2 * lines)
    ]


def layer_one_kernel(
    col_size, points_hbm, slots_hbm, w_in_hbm, w_out_hbm, gate_up_hbm, down_hbm, out, wide,
    inverse, route, held, slot_all, points, w_in, w_out, gate_up, down, loaded, send, recv,
    s_send, s_recv,
):
    rows = out.shape[0]
    count = rows // BALL
    keep = count - RAW
    me, near, far = row_peers()
    other = far + near - me
    loads = [
        pltpu.make_async_copy(source, target, loaded.at[i])
        for i, (source, target) in enumerate(
            (
                (slots_hbm, slot_all.at[me]),
                (points_hbm, points.at[pl.ds(0, rows)]),
                (w_in_hbm.at[0], w_in),
                (w_out_hbm.at[0], w_out),
                (gate_up_hbm.at[0], gate_up),
                (down_hbm.at[0], down),
            )
        )
    ]
    greet((near, far, other), "row")
    for load in loads:
        load.start()
    meet(3)
    gather = RowGather(held, wide, send, recv)

    def raw_copy(c):
        return gather.between(
            0,
            c,
            points_hbm.at[pl.ds(c * BALL, BALL)],
            points.at[pl.ds((c + RAW) * BALL, BALL)],
            far,
        )

    for c in range(keep, count):
        raw_copy(c).start()
    loads[0].wait()

    def slot_copy(kind, block, peer):
        return pltpu.make_async_remote_copy(
            src_ref=slot_all.at[me],
            dst_ref=slot_all.at[block],
            send_sem=s_send.at[kind],
            recv_sem=s_recv.at[kind],
            device_id={"row": peer},
            device_id_type=pl.DeviceIdType.MESH,
        )

    for kind, peer in enumerate((near, far, other)):
        slot_copy(kind, me, peer).start()
    slots = slot_all[me]
    parts = out.shape[1] // LANES
    route[...] = (slots // (rows * col_size) * rows + slots % rows) * parts
    for load in loads[1:]:
        load.wait()

    lines = slot_all.shape[1]
    own_steps = count // PAIR
    sent_steps = keep // PAIR
    span = PAIR * BALL

    def step(s, carry):
        @pl.when(s == own_steps)
        def _():
            for c in range(keep, count):
                raw_copy(c).wait_recv()

        u = points[pl.ds(pl.multiple_of(s * span, span), span), :]
        mixed = (u.astype(F32) + fine_attention(normed(u), w_in[...], w_out[...])).astype(BF16)
        value = ff_sum(mixed, gate_up[...], down[...]).astype(BF16)

        @pl.when(s < own_steps)
        def _():
            out[pl.ds(pl.multiple_of(s * span, span), span), :] = value

        unit = normed(value)
        again = s // own_steps
        block = me + (far - me) * again
        first = s * PAIR - RAW * again
        for i in range(PAIR):
            gather.put(block, first + i, unit[i * BALL:(i + 1) * BALL])

            @pl.when(s < sent_steps)
            def _():
                gather.to_far(first + i)

            @pl.when(s < own_steps)
            def _():
                gather.to_near(first + i)

            @pl.when(s == own_steps)
            def _():
                gather.far_to_near(first + i)

        @pl.when(s >= 1)
        def _():
            for i in range(PAIR):
                gather.from_near((s - 1) * PAIR + i)

        @pl.when(s == 1)
        def _():
            for kind, peer in enumerate((near, far, other)):
                slot_copy(kind, peer, peer).wait()
            mine, theirs = positions(slot_all, (me, far), col_size)
            inverse[:lines] = mine * parts
            inverse[lines:] = theirs * parts

        @pl.when(s >= own_steps - 1)
        def _():
            for i in range(PAIR):
                gather.relay((s - own_steps + 1) * PAIR + i)

        return carry

    lax.fori_loop(0, own_steps + 1, step, 0)
    done = 2 * PAIR
    each(keep, count, gather.from_last)
    each(0, done - 1, gather.from_last)

    def tail(c):
        gather.relay(c)
        gather.from_last(c - 1)

    each(done, keep, tail)
    gather.from_last(keep - 1)

    def end(c):
        gather.copy(1, c, me, near).wait_send()
        gather.copy(2, c, far, near).wait_send()

    each(0, count, end)
    each(0, keep, lambda c: gather.copy(0, c, me, far).wait_send())
    for c in range(keep, count):
        raw_copy(c).wait_send()


def take_rows(wide, index, base, taken):
    parts = taken.shape[0] // BALL
    for i in range(BALL):
        taken[pl.ds(i * parts, parts), :] = wide[pl.ds(index[base + i], parts), :]


def taken_rows(taken):
    parts = taken.shape[0] // BALL
    return jnp.concatenate(
        [taken[pl.ds(t, BALL, stride=parts), :] for t in range(parts)], axis=1
    )


def turn_kernel(source, index, w_in, w_out, wide, held, taken, send, recv):
    rows = held.shape[1]
    count = rows // BALL
    total = 2 * count - SENT
    me, near, far = row_peers()
    greet((near, far), "row")
    gather = RowGather(held, wide, send, recv)

    def fetch(n):
        for i in range(PAIR):
            ball = n + i
            take_rows(source, index, (ball + SENT * (ball // count)) * BALL, taken.at[i])

    def work(n, size):
        u = jnp.concatenate([taken_rows(taken.at[i]) for i in range(size)], axis=0).astype(BF16)
        fetch(jnp.minimum(n + size, total - PAIR))
        value = fine_attention(u, w_in[1], w_out[1]).astype(BF16)

        @pl.when(n == 0)
        def _():
            meet(2)

        for i in range(size):
            ball = n + i
            again = ball // count
            block = me + (far - me) * again
            c = ball + (SENT - count) * again
            gather.put(block, c, value[i * BALL:(i + 1) * BALL])

            @pl.when(ball < SENT)
            def _():
                gather.to_far(c)

            @pl.when(ball < count)
            def _():
                gather.to_near(c)

            @pl.when(ball >= count)
            def _():
                gather.far_to_near(c)

    def receive(ball):
        @pl.when((ball >= 0) & (ball < count))
        def _():
            gather.from_near(ball)

        @pl.when(ball >= count)
        def _():
            gather.from_last(ball + SENT - count)

    due = [ALONE + PAIR * (c + 3) for c in range(SENT)]

    def step(n):
        work(n, PAIR)
        for i in range(PAIR):
            receive(n - PAIR + i)
        for c in range(SENT):
            @pl.when(n == due[c])
            def _():
                gather.relay(c)

    fetch(0)
    each(0, ALONE, lambda n: work(n, 1))
    each(0, (total - ALONE) // PAIR, lambda p: step(ALONE + p * PAIR))
    for c in range(SENT):
        if due[c] >= total:
            gather.relay(c)
    each(count - PAIR, count, gather.from_last)
    each(0, SENT, gather.from_last)

    def end(c):
        gather.copy(1, c, me, near).wait_send()
        gather.copy(2, c, far, near).wait_send()

    each(0, count, end)
    each(0, SENT, lambda c: gather.copy(0, c, me, far).wait_send())


class ColGather:
    def __init__(self, pooled, send, recv):
        self.pooled, self.send, self.recv = pooled, send, recv
        self.pieces = recv.shape[1]
        self.half = self.pieces // 2
        self.piece = pooled.shape[1] // self.pieces
        col = lax.axis_index("col")
        me = col % GROUP
        self.me, self.base = me, col - me
        side, line = me % 2, me // 2
        self.over = 1 - 2 * side
        self.flip = me + self.over
        self.pair = me + 2 - 4 * (line % 2)
        self.across = (GROUP // 2 - 1 - line) * 2 + side
        self.second = side + 4 - 2 * (line // 2)
        self.third = side + 6 - 6 * (line // 2)
        self.inner = (line == 1) | (line == 2)
        self.outer = (line == 0) | (line == 3)

    def copy(self, kind, c, block, peer):
        spot = self.pooled.at[block, pl.ds(c * self.piece, self.piece)]
        return pltpu.make_async_remote_copy(
            src_ref=spot,
            dst_ref=spot,
            send_sem=self.send.at[kind, c],
            recv_sem=self.recv.at[block, c],
            device_id={"col": self.base + peer},
            device_id_type=pl.DeviceIdType.MESH,
        )

    def moves(self, kind):
        return (
            (self.me, self.pair),
            (self.me, self.flip),
            (self.me, self.across),
            (self.pair, self.across),
            (self.second, self.pair),
            (self.third, self.pair),
            (self.pair, self.flip),
            (self.second, self.flip),
            (self.third, self.flip),
            (self.flip, self.pair),
        )[kind]

    def go(self, kind, c):
        self.copy(kind, c, *self.moves(kind)).start()

    def landed(self, block, c):
        self.copy(0, c, block, self.pair).wait_recv()

    def all_landed(self, block):
        each(0, self.pieces, lambda c: self.landed(block, c))

    def own(self, c):
        self.go(0, c)
        self.go(1, c)

        @pl.when(self.inner)
        def _():
            self.go(2, c)

    def pass_pair(self, c):
        self.landed(self.pair, c)

        @pl.when(self.inner)
        def _():
            self.go(3, c)

        @pl.when(c < self.half)
        def _():
            self.go(6, c)

    def pass_second(self, c):
        self.landed(self.second, c)

        @pl.when(self.inner)
        def _():
            self.go(4, c)

        self.go(7, c)

    def pass_third(self, c):
        self.landed(self.third, c)

        @pl.when(self.inner)
        def _():
            self.go(5, c)

        self.go(8, c)

    def pass_flip(self):
        each(self.half, self.pieces, lambda c: self.go(9, c))

    def block_of(self, i):
        order = (
            self.me,
            self.flip,
            self.pair,
            self.second,
            self.second + self.over,
            self.third,
            self.pair + self.over,
            self.third + self.over,
        )
        block = order[0]
        for at in range(1, GROUP):
            block = block + (order[at] - order[at - 1]) * ((i + GROUP - at) // GROUP)
        return block

    def unit(self, i):
        half = self.half * self.piece
        late, last = (i + 2) // GROUP, (i + 1) // GROUP
        low = self.block_of(i - last)
        high = self.block_of(i + late - last)
        spots = (low, half * last), (high, half * (1 - late + last))
        return jnp.concatenate(
            [self.pooled[block, pl.ds(pl.multiple_of(at, half), half), :] for block, at in spots],
            axis=0,
        )

    def before(self, i):
        last = self.pieces - 1

        @pl.when(i == 1)
        def _():
            self.pass_pair(last)

        @pl.when((i == 1) & self.inner)
        def _():
            self.pass_second(last)
            self.pass_third(1)

        @pl.when((i == 1) & self.outer)
        def _():
            self.pass_second(1)

        @pl.when(i == 1)
        def _():
            self.all_landed(self.flip)

        @pl.when((i == 1) & self.outer)
        def _():
            self.pass_flip()

        @pl.when((i == 2) & self.inner)
        def _():
            self.pass_third(2)

        @pl.when((i == 3) & self.inner)
        def _():
            each(3, self.pieces, self.pass_third)
            self.pass_flip()

        @pl.when((i == 3) & self.outer)
        def _():
            each(2, self.pieces, self.pass_second)

        @pl.when((i == 4) & self.outer)
        def _():
            each(0, 2, self.pass_third)

        @pl.when(i == 4)
        def _():
            self.all_landed(self.second + self.over)

        @pl.when((i == 5) & self.outer)
        def _():
            each(2, self.pieces, self.pass_third)

        for late in range(2):
            @pl.when(i == GROUP - 2 + late)
            def _():
                for block in (self.pair + self.over, self.third + self.over):
                    each(
                        late * self.half,
                        (1 + late) * self.half,
                        lambda c: self.landed(block, c),
                    )

    def during(self, c):
        @pl.when(c >= 1)
        def _():
            self.pass_pair(c - 1)

        @pl.when((c >= 1) & self.inner)
        def _():
            self.pass_second(c - 1)

        @pl.when((c == self.pieces - 1) & self.inner)
        def _():
            self.pass_third(0)

        @pl.when((c == self.pieces - 1) & self.outer)
        def _():
            self.pass_second(0)

    def finish(self):
        def sent(kind):
            return lambda c: self.copy(kind, c, *self.moves(kind)).wait_send()

        for kind in (0, 1, 7, 8):
            each(0, self.pieces, sent(kind))
        each(0, self.half, sent(6))
        each(self.half, self.pieces, sent(9))

        @pl.when(self.inner)
        def _():
            for kind in (2, 3, 4, 5):
                each(0, self.pieces, sent(kind))


def layer_two_kernel(
    first, wide, index, gate_up, down, pool, w_in, second, own, mixture, pooled, taken, tall,
    queries, top, value_sum, weight_sum, send, recv
):
    rows = second.shape[0]
    span = PAIR * BALL
    gather = ColGather(pooled, send, recv)
    me, pieces, piece = gather.me, gather.pieces, gather.piece
    greet([gather.base + p for p in (gather.flip, gather.pair, gather.across)], "col")

    def fetch(c):
        for i in range(PAIR):
            take_rows(wide, index, (c * PAIR + i) * BALL, taken.at[i])

    fetch(0)

    def step(c, carry):
        at = pl.multiple_of(c * span, span)
        turned = jnp.concatenate([taken_rows(taken.at[i]) for i in range(PAIR)], axis=0)
        mixed = (first[pl.ds(at, span), :].astype(F32) + turned).astype(BF16)
        fetch(jnp.minimum(c + 1, pieces - 1))
        result = ff_sum(mixed, gate_up[1], down[1]).astype(BF16)
        second[pl.ds(at, span), :] = result
        for t in range(tall.shape[0]):
            tall[t] = result[:, t * LANES:(t + 1) * LANES].astype(F32)
        side = [
            tall[t, pl.ds(j, piece, stride=FAN), :].astype(BF16)
            for j in range(FAN)
            for t in range(tall.shape[0])
        ]
        total = dot(jnp.concatenate(side, axis=1), pool[...])
        pooled[me, pl.ds(pl.multiple_of(c * piece, piece), piece), :] = total.astype(BF16)

        @pl.when(c == 0)
        def _():
            meet(3)

        gather.own(c)
        gather.during(c)
        return carry

    lax.fori_loop(0, pieces, step, 0)
    small, width = own.shape
    size = width // CHEADS
    factor = size ** -0.5 * LOG2E
    part = 2 * LANES
    heads = part // size
    pairs = LANES // size
    head_of = lax.broadcasted_iota(jnp.int32, (small, part), 1) // size
    lane_head = lax.broadcasted_iota(jnp.int32, (small, LANES), 1) // size
    zero, one = jnp.zeros((), BF16), jnp.ones((), BF16)
    own[...] = pooled[me]
    queries[...] = dot(normed(pooled[me]), w_in[:, :width]).astype(BF16)
    top[...] = jnp.full(top.shape, -1e38, F32)
    value_sum[...] = jnp.zeros(value_sum.shape, F32)
    weight_sum[...] = jnp.zeros(weight_sum.shape, F32)

    def attend(i, carry):
        gather.before(i)
        packed = dot(normed(gather.unit(i)), w_in[:, width:]).astype(BF16)
        for g in range(width // part):
            at = g * part
            q = queries[:, at:at + part]
            k = packed[:, at:at + part]
            v = packed[:, width + at:width + at + part]
            results, scales = [], []
            for h in range(heads):
                mine = head_of == h
                s = dot_t(jnp.where(mine, q, zero), k)
                old = top[g * heads + h]
                m = jnp.maximum(old, jnp.max(s, axis=-1, keepdims=True))
                top[g * heads + h] = m
                tiled = jnp.concatenate([m] * (s.shape[1] // LANES), axis=1)
                e = jnp.exp2((s - tiled) * factor).astype(BF16)
                scales.append(jnp.exp2((old - m) * factor))
                results.append(dot(e, jnp.where(mine, v, one)))
            for t in range(part // LANES):
                lane = slice(t * LANES, (t + 1) * LANES)
                free = slice((1 - t) * LANES, (2 - t) * LANES)
                scale, value, total = None, None, None
                for h in range(t * pairs, (t + 1) * pairs):
                    here = (scales[h], results[h][:, lane], results[h][:, free])
                    if scale is None:
                        scale, value, total = here
                    else:
                        pick = lane_head >= h - t * pairs
                        scale = jnp.where(pick, here[0], scale)
                        value = jnp.where(pick, here[1], value)
                        total = jnp.where(pick, here[2], total)
                spot = slice(at + t * LANES, at + (t + 1) * LANES)
                value_sum[:, spot] = value_sum[:, spot] * scale + value
                weight_sum[:, spot] = weight_sum[:, spot] * scale + total
        return carry

    lax.fori_loop(0, GROUP, attend, 0)
    mixture[...] = (value_sum[...] / weight_sum[...]).astype(BF16)
    gather.finish()


def coarse_kernel(pooled, mixture, second, w_out, gate_up, down, unpool, out, lifted):
    rows = pooled.shape[0]
    mixed = (pooled[...].astype(F32) + dot(mixture[...], w_out[...])).astype(BF16)
    coarse = ff_sum(mixed, gate_up[...], down[...]).astype(BF16)
    up = normed(coarse)
    fine = out.shape[1]
    for j in range(FAN):
        part_up = dot(up, unpool[:, j * fine:(j + 1) * fine])
        for t in range(lifted.shape[0]):
            lifted[t, pl.ds(j, rows, stride=FAN), :] = part_up[:, t * LANES:(t + 1) * LANES]
    for c in range(out.shape[0] // BALL):
        at = c * BALL
        for t in range(lifted.shape[0]):
            lane = slice(t * LANES, (t + 1) * LANES)
            out[at:at + BALL, lane] = (
                second[at:at + BALL, lane].astype(F32) + lifted[t, at:at + BALL, :]
            ).astype(BF16)


VMEM = pl.BlockSpec(memory_space=pltpu.VMEM)
SMEM = pl.BlockSpec(memory_space=pltpu.SMEM)
DMA = pltpu.SemaphoreType.DMA


def local(
    points,
    rotated_slot,
    fine_attend_in,
    fine_attend_out,
    fine_gate_up,
    fine_down,
    pool_weight,
    coarse_attend_in,
    coarse_attend_out,
    coarse_gate_up,
    coarse_down,
    unpool_weight,
):
    rows, width = points.shape
    row_size = lax.axis_size("row")
    col_size = lax.axis_size("col")
    count = rows // BALL
    small = rows // FAN
    coarse_width = pool_weight.shape[1]
    lanes = LANES
    lines = rows // lanes
    mib = 1024 * 1024
    parts = width // LANES
    everyone = jax.ShapeDtypeStruct((row_size * rows * parts, LANES), F32)
    held = pltpu.VMEM((row_size, rows, width), BF16)
    scalars = jax.ShapeDtypeStruct((lines, lanes), jnp.int32)
    both = jax.ShapeDtypeStruct((2 * lines, lanes), jnp.int32)

    first, wide, inverse, route = pl.pallas_call(
        functools.partial(layer_one_kernel, col_size),
        out_shape=(jax.ShapeDtypeStruct((rows, width), BF16), everyone, both, scalars),
        in_specs=[pl.BlockSpec(memory_space=pltpu.HBM)] * 6,
        out_specs=(VMEM,) * 4,
        scratch_shapes=[
            held,
            pltpu.VMEM((row_size, lines, lanes), jnp.int32),
            pltpu.VMEM((rows + RAW * BALL, width), BF16),
            pltpu.VMEM(fine_attend_in.shape[1:], BF16),
            pltpu.VMEM(fine_attend_out.shape[1:], BF16),
            pltpu.VMEM(fine_gate_up.shape[1:], BF16),
            pltpu.VMEM(fine_down.shape[1:], BF16),
            DMA((6,)),
            DMA((3, count)),
            DMA((3, count)),
            DMA((3,)),
            DMA((3,)),
        ],
        compiler_params=pltpu.CompilerParams(
            collective_id=0, has_side_effects=True, vmem_limit_bytes=36 * mib
        ),
        name="layer_one",
    )(
        *(
            pltpu.with_memory_space_constraint(array, pltpu.HBM)
            for array in (
                points,
                rotated_slot.reshape(lines, lanes),
                fine_attend_in,
                fine_attend_out,
                fine_gate_up,
                fine_down,
            )
        )
    )

    turned = pl.pallas_call(
        turn_kernel,
        out_shape=everyone,
        in_specs=[VMEM, SMEM, VMEM, VMEM],
        out_specs=VMEM,
        scratch_shapes=[
            held,
            pltpu.VMEM((PAIR, BALL * parts, LANES), F32),
            DMA((3, count)),
            DMA((3, count)),
        ],
        compiler_params=pltpu.CompilerParams(
            collective_id=1, has_side_effects=True, vmem_limit_bytes=24 * mib
        ),
        name="turn",
    )(wide, inverse.reshape(-1), fine_attend_in, fine_attend_out)

    pieces = count // PAIR
    kinds = 10
    one = jax.ShapeDtypeStruct((small, coarse_width), BF16)
    totals = pltpu.VMEM((small, coarse_width), F32)
    second, *coarse_parts = pl.pallas_call(
        layer_two_kernel,
        out_shape=(jax.ShapeDtypeStruct((rows, width), BF16), one, one),
        in_specs=[VMEM, VMEM, SMEM, VMEM, VMEM, VMEM, VMEM],
        out_specs=(VMEM,) * 3,
        scratch_shapes=[
            pltpu.VMEM((GROUP, small, coarse_width), BF16),
            pltpu.VMEM((PAIR, BALL * parts, LANES), F32),
            pltpu.VMEM((parts, PAIR * BALL, LANES), F32),
            pltpu.VMEM((small, coarse_width), BF16),
            pltpu.VMEM((CHEADS, small, LANES), F32),
            totals,
            totals,
            DMA((kinds, pieces)),
            DMA((GROUP, pieces)),
        ],
        compiler_params=pltpu.CompilerParams(
            collective_id=2, has_side_effects=True, vmem_limit_bytes=24 * mib
        ),
        name="layer_two",
    )(first, turned, route.reshape(-1), fine_gate_up, fine_down, pool_weight, coarse_attend_in)

    return pl.pallas_call(
        coarse_kernel,
        out_shape=jax.ShapeDtypeStruct((rows, width), BF16),
        in_specs=[VMEM] * 7,
        out_specs=VMEM,
        scratch_shapes=[
            pltpu.VMEM((width // LANES, rows, LANES), F32),
        ],
        compiler_params=pltpu.CompilerParams(vmem_limit_bytes=22 * mib),
        name="coarse",
    )(
        *coarse_parts,
        second,
        coarse_attend_out,
        coarse_gate_up,
        coarse_down,
        unpool_weight,
    )


def solution(mesh):
    split = P(("row", "col"), None)
    placed = (split, P(("row", "col"))) + (P(),) * 10
    return jax.shard_map(local, mesh=mesh, in_specs=placed, out_specs=split, check_vma=False)
```

```python
import functools
import math

import jax
import jax.numpy as jnp
from jax import lax
from jax.experimental import pallas as pl
from jax.experimental.pallas import tpu as pltpu
from jax.sharding import PartitionSpec as P

HEADS = 8
CHEADS = 8
BALL = 256
GROUP = 8
FAN = 8
LANES = 128
EPS = 1e-06
F32 = jnp.float32
BF16 = jnp.bfloat16
LOG2E = 1.4426950408889634


def dot(a, b):
    return jnp.dot(a, b, preferred_element_type=F32)


def dot_t(a, b):
    return lax.dot_general(a, b, (((1,), (1,)), ((), ())), preferred_element_type=F32)


def normed(x):
    wide = x.astype(F32)
    return (wide * lax.rsqrt(jnp.mean(wide * wide, axis=-1, keepdims=True) + EPS)).astype(BF16)


def ff_sum(x, gate_up, down):
    both = dot(normed(x), gate_up)
    half = both.shape[1] // 2
    g = both[:, :half]
    hidden = ((0.5 * g) * (1.0 + jnp.tanh(0.5 * g)) * both[:, half:]).astype(BF16)
    return x.astype(F32) + dot(hidden, down)


def ff_parts(x, gate_up, down, count):
    n = normed(x)
    half = down.shape[0]
    size = half // count
    total = x.astype(F32)
    for at in range(0, half, size):
        g = dot(n, gate_up[:, at:at + size])
        up = dot(n, gate_up[:, half + at:half + at + size])
        hidden = ((0.5 * g) * (1.0 + jnp.tanh(0.5 * g)) * up).astype(BF16)
        total = total + dot(hidden, down[at:at + size, :])
    return total


def ball_mixture(packed):
    rows, width = packed.shape[0], packed.shape[1] // 3
    q, k, v = packed[:, :width], packed[:, width:2 * width], packed[:, 2 * width:]
    size = width // HEADS
    factor = size ** -0.5 * LOG2E
    half = width // 2
    head_of = lax.broadcasted_iota(jnp.int32, (rows, width), 1) // size
    zero = jnp.zeros((), BF16)
    parts = []
    for g in range(2):
        both = None
        for h in range(g * HEADS // 2, (g + 1) * HEADS // 2):
            mine = head_of == h
            s = dot_t(jnp.where(mine, q, zero), k)
            m = jnp.max(s, axis=-1, keepdims=True)
            e = jnp.exp2((s - m) * factor).astype(BF16)
            mine = mine[:, g * half:(g + 1) * half]
            value = jnp.concatenate(
                (
                    jnp.where(mine, v[:, g * half:(g + 1) * half], zero),
                    jnp.where(mine, jnp.ones((), BF16), zero),
                ),
                axis=1,
            )
            r = dot(e, value)
            both = r if both is None else both + r
        parts.append((both[:, :half] / both[:, half:]).astype(BF16))
    return jnp.concatenate(parts, axis=1)


def fine_attention(n, w_in, w_out):
    packed = dot(n, w_in).astype(BF16)
    balls = [ball_mixture(packed[i:i + BALL]) for i in range(0, n.shape[0], BALL)]
    return dot(jnp.concatenate(balls, axis=0), w_out)


def row_peers():
    me = lax.axis_index("row")
    near = me + 1 - 2 * (me % 2)
    far = me + 2 - 4 * ((me // 2) % 2)
    return me, near, far


def greet(peers, axis):
    barrier = pltpu.get_barrier_semaphore()
    for peer in peers:
        pl.semaphore_signal(
            barrier, inc=1, device_id={axis: peer}, device_id_type=pl.DeviceIdType.MESH
        )


def meet(count):
    pl.semaphore_wait(pltpu.get_barrier_semaphore(), count)


PAIR = 2
RAW = 2
FF_PARTS = 4
SENT = 3
ALONE = 1


class RowGather:
    def __init__(self, held, wide, send, recv):
        self.held, self.wide = held, wide
        self.send, self.recv = send, recv
        self.me, self.near, self.far = row_peers()
        self.last = self.far + self.near - self.me

    def copy(self, kind, c, block, peer):
        spot = self.held.at[block, pl.ds(c * BALL, BALL)]
        return self.between(kind, c, spot, spot, peer)

    def between(self, kind, c, source, target, peer):
        return pltpu.make_async_remote_copy(
            src_ref=source,
            dst_ref=target,
            send_sem=self.send.at[kind, c],
            recv_sem=self.recv.at[kind, c],
            device_id={"row": peer},
            device_id_type=pl.DeviceIdType.MESH,
        )

    def put(self, block, c, value):
        rows = self.held.shape[1]
        self.held[block, pl.ds(pl.multiple_of(c * BALL, BALL), BALL), :] = value
        self.widen(block, c, value)

    def widen(self, block, c, value):
        rows, width = self.held.shape[1:]
        parts = width // LANES
        at = pl.multiple_of((block * rows + c * BALL) * parts, BALL * parts)
        for t in range(parts):
            self.wide[pl.ds(at + t, BALL, stride=parts), :] = value[
                :, t * LANES:(t + 1) * LANES
            ].astype(F32)

    def arrived(self, block, c):
        at = pl.multiple_of(c * BALL, BALL)
        self.widen(block, c, self.held[block, pl.ds(at, BALL), :])

    def to_far(self, c):
        self.copy(0, c, self.me, self.far).start()

    def to_near(self, c):
        self.copy(1, c, self.me, self.near).start()

    def far_to_near(self, c):
        self.copy(2, c, self.far, self.near).start()

    def relay(self, c):
        self.copy(0, c, self.far, self.far).wait_recv()
        self.far_to_near(c)
        self.arrived(self.far, c)

    def from_near(self, c):
        self.copy(1, c, self.near, self.near).wait_recv()
        self.arrived(self.near, c)

    def from_last(self, c):
        self.copy(2, c, self.last, self.near).wait_recv()
        self.arrived(self.last, c)


def each(start, stop, do):
    def body(c, carry):
        do(c)
        return carry

    lax.fori_loop(start, stop, body, 0)


def positions(slot_all, targets, col_size):
    lines, lanes = slot_all.shape[1:]
    rows = lines * lanes
    row_id = lax.broadcasted_iota(jnp.int32, (lines, lanes), 0)
    lane_id = lax.broadcasted_iota(jnp.int32, (lines, lanes), 1).astype(F32)
    sub_id = lax.broadcasted_iota(jnp.int32, (lanes, lanes), 0)
    left, right = [], []
    for r in range(slot_all.shape[0]):
        for c in range(lines):
            line = slot_all[r, c:c + 1, :]
            owner, spot = line // (rows * col_size), line % rows
            parts = []
            for target in targets:
                hit = row_id == jnp.where(owner == target, spot // lanes, lines)
                parts += [jnp.where(hit, float(r * lines + c), 0.0), jnp.where(hit, lane_id, 0.0)]
            left.append(jnp.concatenate(parts, axis=0).astype(BF16))
            right.append(jnp.where(sub_id == spot % lanes, 1.0, 0.0).astype(BF16))
    found = dot_t(jnp.concatenate(left, axis=1), jnp.concatenate(right, axis=1))
    return [
        (found[at:at + lines] * lanes + found[at + lines:at + 2 * lines]).astype(jnp.int32)
        for at in range(0, found.shape[0], 2 * lines)
    ]


def layer_one_kernel(
    col_size, points_hbm, slots_hbm, w_in_hbm, w_out_hbm, gate_up_hbm, down_hbm, out, wide,
    inverse, route, held, slot_all, points, w_in, w_out, gate_up, down, loaded, send, recv,
    s_send, s_recv,
):
    rows = out.shape[0]
    count = rows // BALL
    keep = count - RAW
    me, near, far = row_peers()
    other = far + near - me
    loads = [
        pltpu.make_async_copy(source, target, loaded.at[i])
        for i, (source, target) in enumerate(
            (
                (slots_hbm, slot_all.at[me]),
                (points_hbm, points.at[pl.ds(0, rows)]),
                (w_in_hbm.at[0], w_in),
                (w_out_hbm.at[0], w_out),
                (gate_up_hbm.at[0], gate_up),
                (down_hbm.at[0], down),
            )
        )
    ]
    greet((near, far, other), "row")
    for load in loads:
        load.start()
    meet(3)
    gather = RowGather(held, wide, send, recv)

    def raw_copy(c):
        return gather.between(
            0,
            c,
            points_hbm.at[pl.ds(c * BALL, BALL)],
            points.at[pl.ds((c + RAW) * BALL, BALL)],
            far,
        )

    for c in range(keep, count):
        raw_copy(c).start()
    loads[0].wait()

    def slot_copy(kind, block, peer):
        return pltpu.make_async_remote_copy(
            src_ref=slot_all.at[me],
            dst_ref=slot_all.at[block],
            send_sem=s_send.at[kind],
            recv_sem=s_recv.at[kind],
            device_id={"row": peer},
            device_id_type=pl.DeviceIdType.MESH,
        )

    for kind, peer in enumerate((near, far, other)):
        slot_copy(kind, me, peer).start()
    slots = slot_all[me]
    parts = out.shape[1] // LANES
    route[...] = (slots // (rows * col_size) * rows + slots % rows) * parts
    for load in loads[1:]:
        load.wait()

    lines = slot_all.shape[1]
    own_steps = count // PAIR
    sent_steps = keep // PAIR
    span = PAIR * BALL

    def step(s, carry):
        @pl.when(s == own_steps)
        def _():
            for c in range(keep, count):
                raw_copy(c).wait_recv()

        u = points[pl.ds(pl.multiple_of(s * span, span), span), :]
        mixed = (u.astype(F32) + fine_attention(normed(u), w_in[...], w_out[...])).astype(BF16)
        value = ff_sum(mixed, gate_up[...], down[...]).astype(BF16)

        @pl.when(s < own_steps)
        def _():
            out[pl.ds(pl.multiple_of(s * span, span), span), :] = value

        unit = normed(value)
        again = s // own_steps
        block = me + (far - me) * again
        first = s * PAIR - RAW * again
        for i in range(PAIR):
            gather.put(block, first + i, unit[i * BALL:(i + 1) * BALL])

            @pl.when(s < sent_steps)
            def _():
                gather.to_far(first + i)

            @pl.when(s < own_steps)
            def _():
                gather.to_near(first + i)

            @pl.when(s == own_steps)
            def _():
                gather.far_to_near(first + i)

        @pl.when(s >= 1)
        def _():
            for i in range(PAIR):
                gather.from_near((s - 1) * PAIR + i)

        @pl.when(s == 1)
        def _():
            for kind, peer in enumerate((near, far, other)):
                slot_copy(kind, peer, peer).wait()
            mine, theirs = positions(slot_all, (me, far), col_size)
            inverse[:lines] = mine * parts
            inverse[lines:] = theirs * parts

        @pl.when(s >= own_steps - 1)
        def _():
            for i in range(PAIR):
                gather.relay((s - own_steps + 1) * PAIR + i)

        return carry

    lax.fori_loop(0, own_steps + 1, step, 0)
    done = 2 * PAIR
    each(keep, count, gather.from_last)
    each(0, done - 1, gather.from_last)

    def tail(c):
        gather.relay(c)
        gather.from_last(c - 1)

    each(done, keep, tail)
    gather.from_last(keep - 1)

    def end(c):
        gather.copy(1, c, me, near).wait_send()
        gather.copy(2, c, far, near).wait_send()

    each(0, count, end)
    each(0, keep, lambda c: gather.copy(0, c, me, far).wait_send())
    for c in range(keep, count):
        raw_copy(c).wait_send()


def take_rows(wide, index, base, taken):
    parts = taken.shape[0] // BALL
    for i in range(BALL):
        taken[pl.ds(i * parts, parts), :] = wide[pl.ds(index[base + i], parts), :]


def taken_rows(taken):
    parts = taken.shape[0] // BALL
    return jnp.concatenate(
        [taken[pl.ds(t, BALL, stride=parts), :] for t in range(parts)], axis=1
    )


def turn_kernel(source, index, w_in, w_out, wide, held, taken, send, recv):
    rows = held.shape[1]
    count = rows // BALL
    total = 2 * count - SENT
    me, near, far = row_peers()
    greet((near, far), "row")
    gather = RowGather(held, wide, send, recv)

    def fetch(n):
        for i in range(PAIR):
            ball = n + i
            take_rows(source, index, (ball + SENT * (ball // count)) * BALL, taken.at[i])

    def work(n, size):
        u = jnp.concatenate([taken_rows(taken.at[i]) for i in range(size)], axis=0).astype(BF16)
        fetch(jnp.minimum(n + size, total - PAIR))
        value = fine_attention(u, w_in[1], w_out[1]).astype(BF16)

        @pl.when(n == 0)
        def _():
            meet(2)

        for i in range(size):
            ball = n + i
            again = ball // count
            block = me + (far - me) * again
            c = ball + (SENT - count) * again
            gather.put(block, c, value[i * BALL:(i + 1) * BALL])

            @pl.when(ball < SENT)
            def _():
                gather.to_far(c)

            @pl.when(ball < count)
            def _():
                gather.to_near(c)

            @pl.when(ball >= count)
            def _():
                gather.far_to_near(c)

    def receive(ball):
        @pl.when((ball >= 0) & (ball < count))
        def _():
            gather.from_near(ball)

        @pl.when(ball >= count)
        def _():
            gather.from_last(ball + SENT - count)

    due = [ALONE + PAIR * (c + 3) for c in range(SENT)]

    def step(n):
        work(n, PAIR)
        for i in range(PAIR):
            receive(n - PAIR + i)
        for c in range(SENT):
            @pl.when(n == due[c])
            def _():
                gather.relay(c)

    fetch(0)
    each(0, ALONE, lambda n: work(n, 1))
    each(0, (total - ALONE) // PAIR, lambda p: step(ALONE + p * PAIR))
    for c in range(SENT):
        if due[c] >= total:
            gather.relay(c)
    each(count - PAIR, count, gather.from_last)
    each(0, SENT, gather.from_last)

    def end(c):
        gather.copy(1, c, me, near).wait_send()
        gather.copy(2, c, far, near).wait_send()

    each(0, count, end)
    each(0, SENT, lambda c: gather.copy(0, c, me, far).wait_send())


class ColGather:
    def __init__(self, pooled, send, recv):
        self.pooled, self.send, self.recv = pooled, send, recv
        self.pieces = recv.shape[1]
        self.half = self.pieces // 2
        self.piece = pooled.shape[1] // self.pieces
        col = lax.axis_index("col")
        me = col % GROUP
        self.me, self.base = me, col - me
        side, line = me % 2, me // 2
        self.over = 1 - 2 * side
        self.flip = me + self.over
        self.pair = me + 2 - 4 * (line % 2)
        self.across = (GROUP // 2 - 1 - line) * 2 + side
        self.second = side + 4 - 2 * (line // 2)
        self.third = side + 6 - 6 * (line // 2)
        self.inner = (line == 1) | (line == 2)
        self.outer = (line == 0) | (line == 3)

    def copy(self, kind, c, block, peer):
        spot = self.pooled.at[block, pl.ds(c * self.piece, self.piece)]
        return pltpu.make_async_remote_copy(
            src_ref=spot,
            dst_ref=spot,
            send_sem=self.send.at[kind, c],
            recv_sem=self.recv.at[block, c],
            device_id={"col": self.base + peer},
            device_id_type=pl.DeviceIdType.MESH,
        )

    def moves(self, kind):
        return (
            (self.me, self.pair),
            (self.me, self.flip),
            (self.me, self.across),
            (self.pair, self.across),
            (self.second, self.pair),
            (self.third, self.pair),
            (self.pair, self.flip),
            (self.second, self.flip),
            (self.third, self.flip),
            (self.flip, self.pair),
        )[kind]

    def go(self, kind, c):
        self.copy(kind, c, *self.moves(kind)).start()

    def landed(self, block, c):
        self.copy(0, c, block, self.pair).wait_recv()

    def all_landed(self, block):
        each(0, self.pieces, lambda c: self.landed(block, c))

    def own(self, c):
        self.go(0, c)
        self.go(1, c)

        @pl.when(self.inner)
        def _():
            self.go(2, c)

    def pass_pair(self, c):
        self.landed(self.pair, c)

        @pl.when(self.inner)
        def _():
            self.go(3, c)

        @pl.when(c < self.half)
        def _():
            self.go(6, c)

    def pass_second(self, c):
        self.landed(self.second, c)

        @pl.when(self.inner)
        def _():
            self.go(4, c)

        self.go(7, c)

    def pass_third(self, c):
        self.landed(self.third, c)

        @pl.when(self.inner)
        def _():
            self.go(5, c)

        self.go(8, c)

    def pass_flip(self):
        each(self.half, self.pieces, lambda c: self.go(9, c))

    def block_of(self, i):
        order = (
            self.me,
            self.flip,
            self.pair,
            self.second,
            self.second + self.over,
            self.third,
            self.pair + self.over,
            self.third + self.over,
        )
        block = order[0]
        for at in range(1, GROUP):
            block = block + (order[at] - order[at - 1]) * ((i + GROUP - at) // GROUP)
        return block

    def unit(self, i):
        half = self.half * self.piece
        late, last = (i + 2) // GROUP, (i + 1) // GROUP
        low = self.block_of(i - last)
        high = self.block_of(i + late - last)
        spots = (low, half * last), (high, half * (1 - late + last))
        return jnp.concatenate(
            [self.pooled[block, pl.ds(pl.multiple_of(at, half), half), :] for block, at in spots],
            axis=0,
        )

    def before(self, i):
        last = self.pieces - 1

        @pl.when(i == 1)
        def _():
            self.pass_pair(last)

        @pl.when((i == 1) & self.inner)
        def _():
            self.pass_second(last)
            self.pass_third(1)

        @pl.when((i == 1) & self.outer)
        def _():
            self.pass_second(1)

        @pl.when(i == 1)
        def _():
            self.all_landed(self.flip)

        @pl.when((i == 1) & self.outer)
        def _():
            self.pass_flip()

        @pl.when((i == 2) & self.inner)
        def _():
            self.pass_third(2)

        @pl.when((i == 3) & self.inner)
        def _():
            each(3, self.pieces, self.pass_third)
            self.pass_flip()

        @pl.when((i == 3) & self.outer)
        def _():
            each(2, self.pieces, self.pass_second)

        @pl.when((i == 4) & self.outer)
        def _():
            each(0, 2, self.pass_third)

        @pl.when(i == 4)
        def _():
            self.all_landed(self.second + self.over)

        @pl.when((i == 5) & self.outer)
        def _():
            each(2, self.pieces, self.pass_third)

        for late in range(2):
            @pl.when(i == GROUP - 2 + late)
            def _():
                for block in (self.pair + self.over, self.third + self.over):
                    each(
                        late * self.half,
                        (1 + late) * self.half,
                        lambda c: self.landed(block, c),
                    )

    def during(self, c):
        @pl.when(c >= 1)
        def _():
            self.pass_pair(c - 1)

        @pl.when((c >= 1) & self.inner)
        def _():
            self.pass_second(c - 1)

        @pl.when((c == self.pieces - 1) & self.inner)
        def _():
            self.pass_third(0)

        @pl.when((c == self.pieces - 1) & self.outer)
        def _():
            self.pass_second(0)

    def finish(self):
        def sent(kind):
            return lambda c: self.copy(kind, c, *self.moves(kind)).wait_send()

        for kind in (0, 1, 7, 8):
            each(0, self.pieces, sent(kind))
        each(0, self.half, sent(6))
        each(self.half, self.pieces, sent(9))

        @pl.when(self.inner)
        def _():
            for kind in (2, 3, 4, 5):
                each(0, self.pieces, sent(kind))


def layer_two_kernel(
    first, wide, index, gate_up, down, pool, w_in, second, own, mixture, pooled, taken, tall,
    queries, top, value_sum, weight_sum, send, recv
):
    rows = second.shape[0]
    span = PAIR * BALL
    gather = ColGather(pooled, send, recv)
    me, pieces, piece = gather.me, gather.pieces, gather.piece
    greet([gather.base + p for p in (gather.flip, gather.pair, gather.across)], "col")

    def fetch(c):
        for i in range(PAIR):
            take_rows(wide, index, (c * PAIR + i) * BALL, taken.at[i])

    fetch(0)

    def step(c, carry):
        at = pl.multiple_of(c * span, span)
        turned = jnp.concatenate([taken_rows(taken.at[i]) for i in range(PAIR)], axis=0)
        mixed = (first[pl.ds(at, span), :].astype(F32) + turned).astype(BF16)
        fetch(jnp.minimum(c + 1, pieces - 1))
        result = ff_parts(mixed, gate_up.at[1], down.at[1], FF_PARTS).astype(BF16)
        second[pl.ds(at, span), :] = result
        for t in range(tall.shape[0]):
            tall[t] = result[:, t * LANES:(t + 1) * LANES].astype(F32)
        side = [
            tall[t, pl.ds(j, piece, stride=FAN), :].astype(BF16)
            for j in range(FAN)
            for t in range(tall.shape[0])
        ]
        total = dot(jnp.concatenate(side, axis=1), pool[...])
        pooled[me, pl.ds(pl.multiple_of(c * piece, piece), piece), :] = total.astype(BF16)

        @pl.when(c == 0)
        def _():
            meet(3)

        gather.own(c)
        gather.during(c)
        return carry

    lax.fori_loop(0, pieces, step, 0)
    small, width = own.shape
    size = width // CHEADS
    factor = size ** -0.5 * LOG2E
    part = 2 * LANES
    heads = part // size
    pairs = LANES // size
    head_of = lax.broadcasted_iota(jnp.int32, (small, part), 1) // size
    lane_head = lax.broadcasted_iota(jnp.int32, (small, LANES), 1) // size
    zero, one = jnp.zeros((), BF16), jnp.ones((), BF16)
    own[...] = pooled[me]
    queries[...] = dot(normed(pooled[me]), w_in[:, :width]).astype(BF16)
    top[...] = jnp.full(top.shape, -1e38, F32)
    value_sum[...] = jnp.zeros(value_sum.shape, F32)
    weight_sum[...] = jnp.zeros(weight_sum.shape, F32)

    def attend(i, carry):
        gather.before(i)
        packed = dot(normed(gather.unit(i)), w_in[:, width:]).astype(BF16)
        for g in range(width // part):
            at = g * part
            q = queries[:, at:at + part]
            k = packed[:, at:at + part]
            v = packed[:, width + at:width + at + part]
            results, scales = [], []
            for h in range(heads):
                mine = head_of == h
                s = dot_t(jnp.where(mine, q, zero), k)
                old = top[g * heads + h]
                m = jnp.maximum(old, jnp.max(s, axis=-1, keepdims=True))
                top[g * heads + h] = m
                tiled = jnp.concatenate([m] * (s.shape[1] // LANES), axis=1)
                e = jnp.exp2((s - tiled) * factor).astype(BF16)
                scales.append(jnp.exp2((old - m) * factor))
                results.append(dot(e, jnp.where(mine, v, one)))
            for t in range(part // LANES):
                lane = slice(t * LANES, (t + 1) * LANES)
                free = slice((1 - t) * LANES, (2 - t) * LANES)
                scale, value, total = None, None, None
                for h in range(t * pairs, (t + 1) * pairs):
                    here = (scales[h], results[h][:, lane], results[h][:, free])
                    if scale is None:
                        scale, value, total = here
                    else:
                        pick = lane_head >= h - t * pairs
                        scale = jnp.where(pick, here[0], scale)
                        value = jnp.where(pick, here[1], value)
                        total = jnp.where(pick, here[2], total)
                spot = slice(at + t * LANES, at + (t + 1) * LANES)
                value_sum[:, spot] = value_sum[:, spot] * scale + value
                weight_sum[:, spot] = weight_sum[:, spot] * scale + total
        return carry

    lax.fori_loop(0, GROUP, attend, 0)
    mixture[...] = (value_sum[...] / weight_sum[...]).astype(BF16)
    gather.finish()


def coarse_kernel(pooled, mixture, second, w_out, gate_up, down, unpool, out, lifted):
    rows = pooled.shape[0]
    mixed = (pooled[...].astype(F32) + dot(mixture[...], w_out[...])).astype(BF16)
    coarse = ff_parts(mixed, gate_up, down, 2).astype(BF16)
    up = normed(coarse)
    fine = out.shape[1]
    for j in range(FAN):
        part_up = dot(up, unpool[:, j * fine:(j + 1) * fine])
        for t in range(lifted.shape[0]):
            lifted[t, pl.ds(j, rows, stride=FAN), :] = part_up[:, t * LANES:(t + 1) * LANES]
    for c in range(out.shape[0] // BALL):
        at = c * BALL
        for t in range(lifted.shape[0]):
            lane = slice(t * LANES, (t + 1) * LANES)
            out[at:at + BALL, lane] = (
                second[at:at + BALL, lane].astype(F32) + lifted[t, at:at + BALL, :]
            ).astype(BF16)


VMEM = pl.BlockSpec(memory_space=pltpu.VMEM)
SMEM = pl.BlockSpec(memory_space=pltpu.SMEM)
DMA = pltpu.SemaphoreType.DMA


def local(
    points,
    rotated_slot,
    fine_attend_in,
    fine_attend_out,
    fine_gate_up,
    fine_down,
    pool_weight,
    coarse_attend_in,
    coarse_attend_out,
    coarse_gate_up,
    coarse_down,
    unpool_weight,
):
    rows, width = points.shape
    row_size = lax.axis_size("row")
    col_size = lax.axis_size("col")
    count = rows // BALL
    small = rows // FAN
    coarse_width = pool_weight.shape[1]
    lanes = LANES
    lines = rows // lanes
    mib = 1024 * 1024
    parts = width // LANES
    everyone = jax.ShapeDtypeStruct((row_size * rows * parts, LANES), F32)
    held = pltpu.VMEM((row_size, rows, width), BF16)
    scalars = jax.ShapeDtypeStruct((lines, lanes), jnp.int32)
    both = jax.ShapeDtypeStruct((2 * lines, lanes), jnp.int32)

    first, wide, inverse, route = pl.pallas_call(
        functools.partial(layer_one_kernel, col_size),
        out_shape=(jax.ShapeDtypeStruct((rows, width), BF16), everyone, both, scalars),
        in_specs=[pl.BlockSpec(memory_space=pltpu.HBM)] * 6,
        out_specs=(VMEM,) * 4,
        scratch_shapes=[
            held,
            pltpu.VMEM((row_size, lines, lanes), jnp.int32),
            pltpu.VMEM((rows + RAW * BALL, width), BF16),
            pltpu.VMEM(fine_attend_in.shape[1:], BF16),
            pltpu.VMEM(fine_attend_out.shape[1:], BF16),
            pltpu.VMEM(fine_gate_up.shape[1:], BF16),
            pltpu.VMEM(fine_down.shape[1:], BF16),
            DMA((6,)),
            DMA((3, count)),
            DMA((3, count)),
            DMA((3,)),
            DMA((3,)),
        ],
        compiler_params=pltpu.CompilerParams(
            collective_id=0, has_side_effects=True, vmem_limit_bytes=36 * mib
        ),
        name="layer_one",
    )(
        *(
            pltpu.with_memory_space_constraint(array, pltpu.HBM)
            for array in (
                points,
                rotated_slot.reshape(lines, lanes),
                fine_attend_in,
                fine_attend_out,
                fine_gate_up,
                fine_down,
            )
        )
    )

    turned = pl.pallas_call(
        turn_kernel,
        out_shape=everyone,
        in_specs=[VMEM, SMEM, VMEM, VMEM],
        out_specs=VMEM,
        scratch_shapes=[
            held,
            pltpu.VMEM((PAIR, BALL * parts, LANES), F32),
            DMA((3, count)),
            DMA((3, count)),
        ],
        compiler_params=pltpu.CompilerParams(
            collective_id=1, has_side_effects=True, vmem_limit_bytes=24 * mib
        ),
        name="turn",
    )(wide, inverse.reshape(-1), fine_attend_in, fine_attend_out)

    pieces = count // PAIR
    kinds = 10
    one = jax.ShapeDtypeStruct((small, coarse_width), BF16)
    totals = pltpu.VMEM((small, coarse_width), F32)
    second, *coarse_parts = pl.pallas_call(
        layer_two_kernel,
        out_shape=(jax.ShapeDtypeStruct((rows, width), BF16), one, one),
        in_specs=[VMEM, VMEM, SMEM, VMEM, VMEM, VMEM, VMEM],
        out_specs=(VMEM,) * 3,
        scratch_shapes=[
            pltpu.VMEM((GROUP, small, coarse_width), BF16),
            pltpu.VMEM((PAIR, BALL * parts, LANES), F32),
            pltpu.VMEM((parts, PAIR * BALL, LANES), F32),
            pltpu.VMEM((small, coarse_width), BF16),
            pltpu.VMEM((CHEADS, small, LANES), F32),
            totals,
            totals,
            DMA((kinds, pieces)),
            DMA((GROUP, pieces)),
        ],
        compiler_params=pltpu.CompilerParams(
            collective_id=2, has_side_effects=True, vmem_limit_bytes=24 * mib
        ),
        name="layer_two",
    )(first, turned, route.reshape(-1), fine_gate_up, fine_down, pool_weight, coarse_attend_in)

    return pl.pallas_call(
        coarse_kernel,
        out_shape=jax.ShapeDtypeStruct((rows, width), BF16),
        in_specs=[VMEM] * 7,
        out_specs=VMEM,
        scratch_shapes=[
            pltpu.VMEM((width // LANES, rows, LANES), F32),
        ],
        compiler_params=pltpu.CompilerParams(vmem_limit_bytes=22 * mib),
        name="coarse",
    )(
        *coarse_parts,
        second,
        coarse_attend_out,
        coarse_gate_up,
        coarse_down,
        unpool_weight,
    )


def solution(mesh):
    split = P(("row", "col"), None)
    placed = (split, P(("row", "col"))) + (P(),) * 10
    return jax.shard_map(local, mesh=mesh, in_specs=placed, out_specs=split, check_vma=False)
```

```python
import functools
import math

import jax
import jax.numpy as jnp
from jax import lax
from jax.experimental import pallas as pl
from jax.experimental.pallas import tpu as pltpu
from jax.sharding import PartitionSpec as P

HEADS = 8
CHEADS = 8
BALL = 256
GROUP = 8
FAN = 8
LANES = 128
EPS = 1e-06
F32 = jnp.float32
BF16 = jnp.bfloat16
LOG2E = 1.4426950408889634


def dot(a, b):
    return jnp.dot(a, b, preferred_element_type=F32)


def dot_t(a, b):
    return lax.dot_general(a, b, (((1,), (1,)), ((), ())), preferred_element_type=F32)


def normed(x):
    wide = x.astype(F32)
    return (wide * lax.rsqrt(jnp.mean(wide * wide, axis=-1, keepdims=True) + EPS)).astype(BF16)


def ff_sum(x, gate_up, down):
    both = dot(normed(x), gate_up)
    half = both.shape[1] // 2
    g = both[:, :half]
    hidden = ((0.5 * g) * (1.0 + jnp.tanh(0.5 * g)) * both[:, half:]).astype(BF16)
    return x.astype(F32) + dot(hidden, down)


def ff_parts(x, gate_up, down, count):
    n = normed(x)
    half = down.shape[0]
    size = half // count
    total = x.astype(F32)
    for at in range(0, half, size):
        g = dot(n, gate_up[:, at:at + size])
        up = dot(n, gate_up[:, half + at:half + at + size])
        hidden = ((0.5 * g) * (1.0 + jnp.tanh(0.5 * g)) * up).astype(BF16)
        total = total + dot(hidden, down[at:at + size, :])
    return total


def ball_mixture(packed):
    rows, width = packed.shape[0], packed.shape[1] // 3
    q, k, v = packed[:, :width], packed[:, width:2 * width], packed[:, 2 * width:]
    size = width // HEADS
    factor = size ** -0.5 * LOG2E
    half = width // 2
    head_of = lax.broadcasted_iota(jnp.int32, (rows, width), 1) // size
    zero = jnp.zeros((), BF16)
    parts = []
    for g in range(2):
        both = None
        for h in range(g * HEADS // 2, (g + 1) * HEADS // 2):
            mine = head_of == h
            s = dot_t(jnp.where(mine, q, zero), k)
            m = jnp.max(s, axis=-1, keepdims=True)
            e = jnp.exp2((s - m) * factor).astype(BF16)
            mine = mine[:, g * half:(g + 1) * half]
            value = jnp.concatenate(
                (
                    jnp.where(mine, v[:, g * half:(g + 1) * half], zero),
                    jnp.where(mine, jnp.ones((), BF16), zero),
                ),
                axis=1,
            )
            r = dot(e, value)
            both = r if both is None else both + r
        parts.append((both[:, :half] / both[:, half:]).astype(BF16))
    return jnp.concatenate(parts, axis=1)


def fine_attention(n, w_in, w_out):
    packed = dot(n, w_in).astype(BF16)
    balls = [ball_mixture(packed[i:i + BALL]) for i in range(0, n.shape[0], BALL)]
    return dot(jnp.concatenate(balls, axis=0), w_out)


def row_peers():
    me = lax.axis_index("row")
    near = me + 1 - 2 * (me % 2)
    far = me + 2 - 4 * ((me // 2) % 2)
    return me, near, far


def greet(peers, axis):
    barrier = pltpu.get_barrier_semaphore()
    for peer in peers:
        pl.semaphore_signal(
            barrier, inc=1, device_id={axis: peer}, device_id_type=pl.DeviceIdType.MESH
        )


def meet(count):
    pl.semaphore_wait(pltpu.get_barrier_semaphore(), count)


PAIR = 2
RAW = 2
FF_PARTS = 4
SENT = 3
ALONE = 1


class RowGather:
    def __init__(self, held, wide, send, recv):
        self.held, self.wide = held, wide
        self.send, self.recv = send, recv
        self.me, self.near, self.far = row_peers()
        self.last = self.far + self.near - self.me

    def copy(self, kind, c, block, peer):
        spot = self.held.at[block, pl.ds(c * BALL, BALL)]
        return self.between(kind, c, spot, spot, peer)

    def between(self, kind, c, source, target, peer):
        return pltpu.make_async_remote_copy(
            src_ref=source,
            dst_ref=target,
            send_sem=self.send.at[kind, c],
            recv_sem=self.recv.at[kind, c],
            device_id={"row": peer},
            device_id_type=pl.DeviceIdType.MESH,
        )

    def put(self, block, c, value):
        rows = self.held.shape[1]
        self.held[block, pl.ds(pl.multiple_of(c * BALL, BALL), BALL), :] = value
        self.widen(block, c, value)

    def widen(self, block, c, value):
        rows, width = self.held.shape[1:]
        parts = width // LANES
        at = pl.multiple_of((block * rows + c * BALL) * parts, BALL * parts)
        for t in range(parts):
            self.wide[pl.ds(at + t, BALL, stride=parts), :] = value[
                :, t * LANES:(t + 1) * LANES
            ].astype(F32)

    def arrived(self, block, c):
        at = pl.multiple_of(c * BALL, BALL)
        self.widen(block, c, self.held[block, pl.ds(at, BALL), :])

    def to_far(self, c):
        self.copy(0, c, self.me, self.far).start()

    def to_near(self, c):
        self.copy(1, c, self.me, self.near).start()

    def far_to_near(self, c):
        self.copy(2, c, self.far, self.near).start()

    def relay(self, c):
        self.copy(0, c, self.far, self.far).wait_recv()
        self.far_to_near(c)
        self.arrived(self.far, c)

    def from_near(self, c):
        self.copy(1, c, self.near, self.near).wait_recv()
        self.arrived(self.near, c)

    def from_last(self, c):
        self.copy(2, c, self.last, self.near).wait_recv()
        self.arrived(self.last, c)


def each(start, stop, do):
    def body(c, carry):
        do(c)
        return carry

    lax.fori_loop(start, stop, body, 0)


def positions(slot_all, targets, col_size):
    lines, lanes = slot_all.shape[1:]
    rows = lines * lanes
    row_id = lax.broadcasted_iota(jnp.int32, (lines, lanes), 0)
    lane_id = lax.broadcasted_iota(jnp.int32, (lines, lanes), 1).astype(F32)
    sub_id = lax.broadcasted_iota(jnp.int32, (lanes, lanes), 0)
    left, right = [], []
    for r in range(slot_all.shape[0]):
        for c in range(lines):
            line = slot_all[r, c:c + 1, :]
            owner, spot = line // (rows * col_size), line % rows
            parts = []
            for target in targets:
                hit = row_id == jnp.where(owner == target, spot // lanes, lines)
                parts += [jnp.where(hit, float(r * lines + c), 0.0), jnp.where(hit, lane_id, 0.0)]
            left.append(jnp.concatenate(parts, axis=0).astype(BF16))
            right.append(jnp.where(sub_id == spot % lanes, 1.0, 0.0).astype(BF16))
    found = dot_t(jnp.concatenate(left, axis=1), jnp.concatenate(right, axis=1))
    return [
        (found[at:at + lines] * lanes + found[at + lines:at + 2 * lines]).astype(jnp.int32)
        for at in range(0, found.shape[0], 2 * lines)
    ]


def layer_one_kernel(
    col_size, points_hbm, slots_hbm, w_in_hbm, w_out_hbm, gate_up_hbm, down_hbm, out, wide,
    inverse, route, held, slot_all, points, w_in, w_out, gate_up, down, loaded, send, recv,
    s_send, s_recv,
):
    rows = out.shape[0]
    count = rows // BALL
    keep = count - RAW
    me, near, far = row_peers()
    other = far + near - me
    loads = [
        pltpu.make_async_copy(source, target, loaded.at[i])
        for i, (source, target) in enumerate(
            (
                (slots_hbm, slot_all.at[me]),
                (points_hbm, points.at[pl.ds(0, rows)]),
                (w_in_hbm.at[0], w_in),
                (w_out_hbm.at[0], w_out),
                (gate_up_hbm.at[0], gate_up),
                (down_hbm.at[0], down),
            )
        )
    ]
    greet((near, far, other), "row")
    for load in loads:
        load.start()
    meet(3)
    gather = RowGather(held, wide, send, recv)

    def raw_copy(c):
        return gather.between(
            0,
            c,
            points_hbm.at[pl.ds(c * BALL, BALL)],
            points.at[pl.ds((c + RAW) * BALL, BALL)],
            far,
        )

    for c in range(keep, count):
        raw_copy(c).start()
    loads[0].wait()

    def slot_copy(kind, block, peer):
        return pltpu.make_async_remote_copy(
            src_ref=slot_all.at[me],
            dst_ref=slot_all.at[block],
            send_sem=s_send.at[kind],
            recv_sem=s_recv.at[kind],
            device_id={"row": peer},
            device_id_type=pl.DeviceIdType.MESH,
        )

    for kind, peer in enumerate((near, far, other)):
        slot_copy(kind, me, peer).start()
    slots = slot_all[me]
    parts = out.shape[1] // LANES
    route[...] = (slots // (rows * col_size) * rows + slots % rows) * parts
    for load in loads[1:]:
        load.wait()

    lines = slot_all.shape[1]
    own_steps = count // PAIR
    sent_steps = keep // PAIR
    span = PAIR * BALL

    def step(s, carry):
        @pl.when(s == own_steps)
        def _():
            for c in range(keep, count):
                raw_copy(c).wait_recv()

        u = points[pl.ds(pl.multiple_of(s * span, span), span), :]
        mixed = (u.astype(F32) + fine_attention(normed(u), w_in[...], w_out[...])).astype(BF16)
        value = ff_sum(mixed, gate_up[...], down[...]).astype(BF16)

        @pl.when(s < own_steps)
        def _():
            out[pl.ds(pl.multiple_of(s * span, span), span), :] = value

        unit = normed(value)
        again = s // own_steps
        block = me + (far - me) * again
        first = s * PAIR - RAW * again
        for i in range(PAIR):
            gather.put(block, first + i, unit[i * BALL:(i + 1) * BALL])

            @pl.when(s < sent_steps)
            def _():
                gather.to_far(first + i)

            @pl.when(s < own_steps)
            def _():
                gather.to_near(first + i)

            @pl.when(s == own_steps)
            def _():
                gather.far_to_near(first + i)

        @pl.when(s >= 1)
        def _():
            for i in range(PAIR):
                gather.from_near((s - 1) * PAIR + i)

        @pl.when(s == 1)
        def _():
            for kind, peer in enumerate((near, far, other)):
                slot_copy(kind, peer, peer).wait()
            mine, theirs = positions(slot_all, (me, far), col_size)
            inverse[:lines] = mine * parts
            inverse[lines:] = theirs * parts

        @pl.when(s >= own_steps - 1)
        def _():
            for i in range(PAIR):
                gather.relay((s - own_steps + 1) * PAIR + i)

        return carry

    lax.fori_loop(0, own_steps + 1, step, 0)
    done = 2 * PAIR
    each(keep, count, gather.from_last)
    each(0, done - 1, gather.from_last)

    def tail(c):
        gather.relay(c)
        gather.from_last(c - 1)

    each(done, keep, tail)
    gather.from_last(keep - 1)

    def end(c):
        gather.copy(1, c, me, near).wait_send()
        gather.copy(2, c, far, near).wait_send()

    each(0, count, end)
    each(0, keep, lambda c: gather.copy(0, c, me, far).wait_send())
    for c in range(keep, count):
        raw_copy(c).wait_send()


def take_rows(wide, index, base, taken):
    parts = taken.shape[0] // BALL
    for i in range(BALL):
        taken[pl.ds(i * parts, parts), :] = wide[pl.ds(index[base + i], parts), :]


def taken_rows(taken):
    parts = taken.shape[0] // BALL
    return jnp.concatenate(
        [taken[pl.ds(t, BALL, stride=parts), :] for t in range(parts)], axis=1
    )


def turn_kernel(source, index, w_in, w_out, wide, held, taken, send, recv):
    rows = held.shape[1]
    count = rows // BALL
    total = 2 * count - SENT
    me, near, far = row_peers()
    greet((near, far), "row")
    gather = RowGather(held, wide, send, recv)

    def fetch(n):
        for i in range(PAIR):
            ball = n + i
            take_rows(source, index, (ball + SENT * (ball // count)) * BALL, taken.at[i])

    def work(n, size):
        u = jnp.concatenate([taken_rows(taken.at[i]) for i in range(size)], axis=0).astype(BF16)
        fetch(jnp.minimum(n + size, total - PAIR))
        value = fine_attention(u, w_in[1], w_out[1]).astype(BF16)

        @pl.when(n == 0)
        def _():
            meet(2)

        for i in range(size):
            ball = n + i
            again = ball // count
            block = me + (far - me) * again
            c = ball + (SENT - count) * again
            gather.put(block, c, value[i * BALL:(i + 1) * BALL])

            @pl.when(ball < SENT)
            def _():
                gather.to_far(c)

            @pl.when(ball < count)
            def _():
                gather.to_near(c)

            @pl.when(ball >= count)
            def _():
                gather.far_to_near(c)

    def receive(ball):
        @pl.when((ball >= 0) & (ball < count))
        def _():
            gather.from_near(ball)

        @pl.when(ball >= count)
        def _():
            gather.from_last(ball + SENT - count)

    due = [ALONE + PAIR * (c + 3) for c in range(SENT)]

    def step(n):
        work(n, PAIR)
        for i in range(PAIR):
            receive(n - PAIR + i)
        for c in range(SENT):
            @pl.when(n == due[c])
            def _():
                gather.relay(c)

    fetch(0)
    each(0, ALONE, lambda n: work(n, 1))
    each(0, (total - ALONE) // PAIR, lambda p: step(ALONE + p * PAIR))
    for c in range(SENT):
        if due[c] >= total:
            gather.relay(c)
    each(count - PAIR, count, gather.from_last)
    each(0, SENT, gather.from_last)

    def end(c):
        gather.copy(1, c, me, near).wait_send()
        gather.copy(2, c, far, near).wait_send()

    each(0, count, end)
    each(0, SENT, lambda c: gather.copy(0, c, me, far).wait_send())


class ColGather:
    def __init__(self, pooled, send, recv):
        self.pooled, self.send, self.recv = pooled, send, recv
        self.pieces = recv.shape[1]
        self.half = self.pieces // 2
        self.piece = pooled.shape[1] // self.pieces
        col = lax.axis_index("col")
        me = col % GROUP
        self.me, self.base = me, col - me
        side, line = me % 2, me // 2
        self.over = 1 - 2 * side
        self.flip = me + self.over
        self.pair = me + 2 - 4 * (line % 2)
        self.across = (GROUP // 2 - 1 - line) * 2 + side
        self.second = side + 4 - 2 * (line // 2)
        self.third = side + 6 - 6 * (line // 2)
        self.inner = (line == 1) | (line == 2)
        self.outer = (line == 0) | (line == 3)

    def copy(self, kind, c, block, peer):
        spot = self.pooled.at[block, pl.ds(c * self.piece, self.piece)]
        return pltpu.make_async_remote_copy(
            src_ref=spot,
            dst_ref=spot,
            send_sem=self.send.at[kind, c],
            recv_sem=self.recv.at[block, c],
            device_id={"col": self.base + peer},
            device_id_type=pl.DeviceIdType.MESH,
        )

    def moves(self, kind):
        return (
            (self.me, self.pair),
            (self.me, self.flip),
            (self.me, self.across),
            (self.pair, self.across),
            (self.second, self.pair),
            (self.third, self.pair),
            (self.pair, self.flip),
            (self.second, self.flip),
            (self.third, self.flip),
            (self.flip, self.pair),
        )[kind]

    def go(self, kind, c):
        self.copy(kind, c, *self.moves(kind)).start()

    def landed(self, block, c):
        self.copy(0, c, block, self.pair).wait_recv()

    def all_landed(self, block):
        each(0, self.pieces, lambda c: self.landed(block, c))

    def own(self, c):
        self.go(0, c)
        self.go(1, c)

        @pl.when(self.inner)
        def _():
            self.go(2, c)

    def pass_pair(self, c):
        self.landed(self.pair, c)

        @pl.when(self.inner)
        def _():
            self.go(3, c)

        @pl.when(c < self.half)
        def _():
            self.go(6, c)

    def pass_second(self, c):
        self.landed(self.second, c)

        @pl.when(self.inner)
        def _():
            self.go(4, c)

        self.go(7, c)

    def pass_third(self, c):
        self.landed(self.third, c)

        @pl.when(self.inner)
        def _():
            self.go(5, c)

        self.go(8, c)

    def pass_flip(self):
        each(self.half, self.pieces, lambda c: self.go(9, c))

    def block_of(self, i):
        order = (
            self.me,
            self.flip,
            self.pair,
            self.second,
            self.second + self.over,
            self.third,
            self.pair + self.over,
            self.third + self.over,
        )
        block = order[0]
        for at in range(1, GROUP):
            block = block + (order[at] - order[at - 1]) * ((i + GROUP - at) // GROUP)
        return block

    def unit(self, i):
        half = self.half * self.piece
        late, last = (i + 2) // GROUP, (i + 1) // GROUP
        low = self.block_of(i - last)
        high = self.block_of(i + late - last)
        spots = (low, half * last), (high, half * (1 - late + last))
        return jnp.concatenate(
            [self.pooled[block, pl.ds(pl.multiple_of(at, half), half), :] for block, at in spots],
            axis=0,
        )

    def before(self, i):
        last = self.pieces - 1

        @pl.when(i == 1)
        def _():
            self.pass_pair(last)

        @pl.when((i == 1) & self.inner)
        def _():
            self.pass_second(last)
            self.pass_third(1)

        @pl.when((i == 1) & self.outer)
        def _():
            self.pass_second(1)

        @pl.when(i == 1)
        def _():
            self.all_landed(self.flip)

        @pl.when((i == 1) & self.outer)
        def _():
            self.pass_flip()

        @pl.when((i == 2) & self.inner)
        def _():
            self.pass_third(2)

        @pl.when((i == 3) & self.inner)
        def _():
            each(3, self.pieces, self.pass_third)
            self.pass_flip()

        @pl.when((i == 3) & self.outer)
        def _():
            each(2, self.pieces, self.pass_second)

        @pl.when((i == 4) & self.outer)
        def _():
            each(0, 2, self.pass_third)

        @pl.when(i == 4)
        def _():
            self.all_landed(self.second + self.over)

        @pl.when((i == 5) & self.outer)
        def _():
            each(2, self.pieces, self.pass_third)

        for late in range(2):
            @pl.when(i == GROUP - 2 + late)
            def _():
                for block in (self.pair + self.over, self.third + self.over):
                    each(
                        late * self.half,
                        (1 + late) * self.half,
                        lambda c: self.landed(block, c),
                    )

    def during(self, c):
        @pl.when(c >= 1)
        def _():
            self.pass_pair(c - 1)

        @pl.when((c >= 1) & self.inner)
        def _():
            self.pass_second(c - 1)

        @pl.when((c == self.pieces - 1) & self.inner)
        def _():
            self.pass_third(0)

        @pl.when((c == self.pieces - 1) & self.outer)
        def _():
            self.pass_second(0)

    def finish(self):
        def sent(kind):
            return lambda c: self.copy(kind, c, *self.moves(kind)).wait_send()

        for kind in (0, 1, 7, 8):
            each(0, self.pieces, sent(kind))
        each(0, self.half, sent(6))
        each(self.half, self.pieces, sent(9))

        @pl.when(self.inner)
        def _():
            for kind in (2, 3, 4, 5):
                each(0, self.pieces, sent(kind))


def layer_two_kernel(
    first, wide, index, gate_up, down, pool, w_in, second, own, mixture, pooled, taken, tall,
    queries, top, value_sum, weight_sum, send, recv
):
    rows = second.shape[0]
    span = PAIR * BALL
    gather = ColGather(pooled, send, recv)
    me, pieces, piece = gather.me, gather.pieces, gather.piece
    greet([gather.base + p for p in (gather.flip, gather.pair, gather.across)], "col")

    def fetch(c):
        for i in range(PAIR):
            take_rows(wide, index, (c * PAIR + i) * BALL, taken.at[i])

    fetch(0)

    def step(c, carry):
        at = pl.multiple_of(c * span, span)
        turned = jnp.concatenate([taken_rows(taken.at[i]) for i in range(PAIR)], axis=0)
        mixed = (first[pl.ds(at, span), :].astype(F32) + turned).astype(BF16)
        fetch(jnp.minimum(c + 1, pieces - 1))
        result = ff_parts(mixed, gate_up.at[1], down.at[1], FF_PARTS).astype(BF16)
        second[pl.ds(at, span), :] = result
        for t in range(tall.shape[0]):
            tall[t] = result[:, t * LANES:(t + 1) * LANES].astype(F32)
        side = [
            tall[t, pl.ds(j, piece, stride=FAN), :].astype(BF16)
            for j in range(FAN)
            for t in range(tall.shape[0])
        ]
        total = dot(jnp.concatenate(side, axis=1), pool[...])
        pooled[me, pl.ds(pl.multiple_of(c * piece, piece), piece), :] = total.astype(BF16)

        @pl.when(c == 0)
        def _():
            meet(3)

        gather.own(c)
        gather.during(c)
        return carry

    lax.fori_loop(0, pieces, step, 0)
    small, width = own.shape
    size = width // CHEADS
    factor = size ** -0.5 * LOG2E
    part = 2 * LANES
    heads = part // size
    pairs = LANES // size
    head_of = lax.broadcasted_iota(jnp.int32, (small, part), 1) // size
    lane_head = lax.broadcasted_iota(jnp.int32, (small, LANES), 1) // size
    zero, one = jnp.zeros((), BF16), jnp.ones((), BF16)
    own[...] = pooled[me]
    queries[...] = dot(normed(pooled[me]), w_in[:, :width]).astype(BF16)
    top[...] = jnp.full(top.shape, -1e38, F32)
    value_sum[...] = jnp.zeros(value_sum.shape, F32)
    weight_sum[...] = jnp.zeros(weight_sum.shape, F32)

    def attend(i, carry):
        gather.before(i)
        packed = dot(normed(gather.unit(i)), w_in[:, width:]).astype(BF16)
        for g in range(width // part):
            at = g * part
            q = queries[:, at:at + part]
            k = packed[:, at:at + part]
            v = packed[:, width + at:width + at + part]
            results, scales = [], []
            for h in range(heads):
                mine = head_of == h
                s = dot_t(jnp.where(mine, q, zero), k)
                old = top[g * heads + h]
                m = jnp.maximum(old, jnp.max(s, axis=-1, keepdims=True))
                top[g * heads + h] = m
                tiled = jnp.concatenate([m] * (s.shape[1] // LANES), axis=1)
                e = jnp.exp2((s - tiled) * factor).astype(BF16)
                scales.append(jnp.exp2((old - m) * factor))
                results.append(dot(e, jnp.where(mine, v, one)))
            for t in range(part // LANES):
                lane = slice(t * LANES, (t + 1) * LANES)
                free = slice((1 - t) * LANES, (2 - t) * LANES)
                scale, value, total = None, None, None
                for h in range(t * pairs, (t + 1) * pairs):
                    here = (scales[h], results[h][:, lane], results[h][:, free])
                    if scale is None:
                        scale, value, total = here
                    else:
                        pick = lane_head >= h - t * pairs
                        scale = jnp.where(pick, here[0], scale)
                        value = jnp.where(pick, here[1], value)
                        total = jnp.where(pick, here[2], total)
                spot = slice(at + t * LANES, at + (t + 1) * LANES)
                value_sum[:, spot] = value_sum[:, spot] * scale + value
                weight_sum[:, spot] = weight_sum[:, spot] * scale + total
        return carry

    lax.fori_loop(0, GROUP, attend, 0)
    mixture[...] = (value_sum[...] / weight_sum[...]).astype(BF16)
    gather.finish()


def coarse_kernel(
    pooled, mixture, second, w_out, gate_up, down, unpool, result, lifted, out, stored
):
    rows = pooled.shape[0]
    mixed = (pooled[...].astype(F32) + dot(mixture[...], w_out[...])).astype(BF16)
    coarse = ff_parts(mixed, gate_up, down, 2).astype(BF16)
    up = normed(coarse)
    fine = out.shape[1]
    for j in range(FAN):
        part_up = dot(up, unpool[:, j * fine:(j + 1) * fine])
        for t in range(lifted.shape[0]):
            lifted[t, pl.ds(j, rows, stride=FAN), :] = part_up[:, t * LANES:(t + 1) * LANES]
    stores = []
    for c in range(out.shape[0] // BALL):
        at = c * BALL
        for t in range(lifted.shape[0]):
            lane = slice(t * LANES, (t + 1) * LANES)
            out[at:at + BALL, lane] = (
                second[at:at + BALL, lane].astype(F32) + lifted[t, at:at + BALL, :]
            ).astype(BF16)
        spot = pl.ds(at, BALL)
        store = pltpu.make_async_copy(out.at[spot], result.at[spot], stored.at[c])
        store.start()
        stores.append(store)
    for store in stores:
        store.wait()


VMEM = pl.BlockSpec(memory_space=pltpu.VMEM)
SMEM = pl.BlockSpec(memory_space=pltpu.SMEM)
DMA = pltpu.SemaphoreType.DMA


def local(
    points,
    rotated_slot,
    fine_attend_in,
    fine_attend_out,
    fine_gate_up,
    fine_down,
    pool_weight,
    coarse_attend_in,
    coarse_attend_out,
    coarse_gate_up,
    coarse_down,
    unpool_weight,
):
    rows, width = points.shape
    row_size = lax.axis_size("row")
    col_size = lax.axis_size("col")
    count = rows // BALL
    small = rows // FAN
    coarse_width = pool_weight.shape[1]
    lanes = LANES
    lines = rows // lanes
    mib = 1024 * 1024
    parts = width // LANES
    everyone = jax.ShapeDtypeStruct((row_size * rows * parts, LANES), F32)
    held = pltpu.VMEM((row_size, rows, width), BF16)
    scalars = jax.ShapeDtypeStruct((lines, lanes), jnp.int32)
    both = jax.ShapeDtypeStruct((2 * lines, lanes), jnp.int32)

    first, wide, inverse, route = pl.pallas_call(
        functools.partial(layer_one_kernel, col_size),
        out_shape=(jax.ShapeDtypeStruct((rows, width), BF16), everyone, both, scalars),
        in_specs=[pl.BlockSpec(memory_space=pltpu.HBM)] * 6,
        out_specs=(VMEM,) * 4,
        scratch_shapes=[
            held,
            pltpu.VMEM((row_size, lines, lanes), jnp.int32),
            pltpu.VMEM((rows + RAW * BALL, width), BF16),
            pltpu.VMEM(fine_attend_in.shape[1:], BF16),
            pltpu.VMEM(fine_attend_out.shape[1:], BF16),
            pltpu.VMEM(fine_gate_up.shape[1:], BF16),
            pltpu.VMEM(fine_down.shape[1:], BF16),
            DMA((6,)),
            DMA((3, count)),
            DMA((3, count)),
            DMA((3,)),
            DMA((3,)),
        ],
        compiler_params=pltpu.CompilerParams(
            collective_id=0, has_side_effects=True, vmem_limit_bytes=36 * mib
        ),
        name="layer_one",
    )(
        *(
            pltpu.with_memory_space_constraint(array, pltpu.HBM)
            for array in (
                points,
                rotated_slot.reshape(lines, lanes),
                fine_attend_in,
                fine_attend_out,
                fine_gate_up,
                fine_down,
            )
        )
    )

    turned = pl.pallas_call(
        turn_kernel,
        out_shape=everyone,
        in_specs=[VMEM, SMEM, VMEM, VMEM],
        out_specs=VMEM,
        scratch_shapes=[
            held,
            pltpu.VMEM((PAIR, BALL * parts, LANES), F32),
            DMA((3, count)),
            DMA((3, count)),
        ],
        compiler_params=pltpu.CompilerParams(
            collective_id=1, has_side_effects=True, vmem_limit_bytes=24 * mib
        ),
        name="turn",
    )(wide, inverse.reshape(-1), fine_attend_in, fine_attend_out)

    pieces = count // PAIR
    kinds = 10
    one = jax.ShapeDtypeStruct((small, coarse_width), BF16)
    totals = pltpu.VMEM((small, coarse_width), F32)
    second, *coarse_parts = pl.pallas_call(
        layer_two_kernel,
        out_shape=(jax.ShapeDtypeStruct((rows, width), BF16), one, one),
        in_specs=[VMEM, VMEM, SMEM, VMEM, VMEM, VMEM, VMEM],
        out_specs=(VMEM,) * 3,
        scratch_shapes=[
            pltpu.VMEM((GROUP, small, coarse_width), BF16),
            pltpu.VMEM((PAIR, BALL * parts, LANES), F32),
            pltpu.VMEM((parts, PAIR * BALL, LANES), F32),
            pltpu.VMEM((small, coarse_width), BF16),
            pltpu.VMEM((CHEADS, small, LANES), F32),
            totals,
            totals,
            DMA((kinds, pieces)),
            DMA((GROUP, pieces)),
        ],
        compiler_params=pltpu.CompilerParams(
            collective_id=2, has_side_effects=True, vmem_limit_bytes=24 * mib
        ),
        name="layer_two",
    )(first, turned, route.reshape(-1), fine_gate_up, fine_down, pool_weight, coarse_attend_in)

    return pl.pallas_call(
        coarse_kernel,
        out_shape=jax.ShapeDtypeStruct((rows, width), BF16),
        in_specs=[VMEM] * 7,
        out_specs=pl.BlockSpec(memory_space=pltpu.HBM),
        scratch_shapes=[
            pltpu.VMEM((width // LANES, rows, LANES), F32),
            pltpu.VMEM((rows, width), BF16),
            DMA((count,)),
        ],
        compiler_params=pltpu.CompilerParams(vmem_limit_bytes=22 * mib),
        name="coarse",
    )(
        *coarse_parts,
        second,
        coarse_attend_out,
        coarse_gate_up,
        coarse_down,
        unpool_weight,
    )


def solution(mesh):
    split = P(("row", "col"), None)
    placed = (split, P(("row", "col"))) + (P(),) * 10
    return jax.shard_map(local, mesh=mesh, in_specs=placed, out_specs=split, check_vma=False)
```
